32 devices in a mesh: groups: 2 (over y), sec: 4 (over z), tile: 2 (over x), row: 2 (over core).
Axes of the slice: x: 2, y: 2, z: 4, core: 2. Of those that a mesh axis runs over, the one named last changes fastest.
Arguments:
- section_pixels: float32 [8, 512, 4096], P(('groups', 'sec'), ('tile', 'row')), parts along dimension 0, may hold values from -40 to 40
- jitter_index: int32 [8, 512], P(('groups', 'sec'), ('tile', 'row')), parts along dimension 0, may hold values from 0 to 7
- drift_list: int32 [8, 4, 8, 3], P(('groups', 'sec')), parts along dimension 0, may hold values from 0 to 31, as said below
- blend_weight: float32 [8, 4, 8], P(('groups', 'sec')), parts along dimension 0, may hold values from 0.5 to 2
- patch_col: int32 [4, 8], P(('tile', 'row'), 'groups'), parts along dimension 1, may hold values from 0 to 896
Outputs:
- jitter_phase: float32 [8, 512], P(('groups', 'sec'), ('tile', 'row')), parts along dimension 0
- surfaces: float32 [6, 4, 4, 128, 128], P('groups', ('tile', 'row'), 'sec'), parts along dimension 0
The draws below stay inside these ranges and needn't reach their ends.
There are 2 independent parts, one for each index of `groups`. The reference program is written for one: setup_inputs(seed, part) draws one part's arguments, and reference() takes and returns one part's arrays. A program takes and returns all parts, laid end to end along the dimension named above; each array names one. Nothing has to cross between parts.
Inputs may be any that keep to these rules, and one draw needn't show every extreme that they name: `drift_list`: entry [s, j, k] names a block of band j (distinct over k), the band that owns its target, and the target block. No band sends more than 2 blocks to one owner, and in every section one owner receives exactly 2 blocks from every band.
All inputs are finite; a program needn't handle non-finite values.
Results may differ from the reference program's by a relative error of at most 0.0065.
Values may be sent and summed in bfloat16 or wider, within the bound.
A program may use at most 64 MiB of HBM per device.

```python
import math
import jax
import jax.numpy as jnp
from jax import lax

W = 4096
SEG = 512
PATCH = 128
BLOCK = 128
JMAX = 8
OV = 8
CAP = 2
ROWS_DEV = 128
SECTIONS = 4
OWNERS = 4
ROWS = 512
NBLK = 32
N_SEC = 4


def coarse_delays(key):
    return jax.random.randint(jax.random.fold_in(key, 11), (SECTIONS, ROWS), 0, JMAX).astype(jnp.int32)


def draw_jitter_index(key, part):
    return coarse_delays(key)


def draw_section_pixels(key, part):
    delays = coarse_delays(key)
    span_cols = W + JMAX + 1
    shared = jax.random.normal(jax.random.fold_in(key, 21), (1, ROWS + 1, span_cols), jnp.float32)
    own_field = jax.random.normal(jax.random.fold_in(key, 22), (SECTIONS, ROWS + 1, span_cols), jnp.float32)
    field_sum = 0.3 * shared + own_field
    mixed = (field_sum[:, 1:] + field_sum[:, :-1]) * 0.7071
    fraction = jax.random.uniform(jax.random.fold_in(key, 23), (SECTIONS, ROWS, 1), jnp.float32)
    columns = jnp.arange(W, dtype=jnp.int32)[None, None, :] - delays[:, :, None] + JMAX
    first_pick = jnp.take_along_axis(mixed, columns, 2)
    second_pick = jnp.take_along_axis(mixed, columns + 1, 2)
    noise_part = jax.random.normal(jax.random.fold_in(key, 24), (SECTIONS, ROWS, W), jnp.float32)
    picture = (1.0 - fraction) * first_pick + fraction * second_pick + 0.3 * noise_part
    return jnp.clip(picture, -40.0, 40.0)


def draw_drift_list(key, part):
    slot_count = OWNERS * CAP

    def one_band(band_key, hot_owner):
        perm_key, source_key, target_key, order_key = jax.random.split(band_key, 4)
        ordering = jax.random.permutation(perm_key, slot_count)
        placing = jnp.argsort(ordering)
        slot_ids = jnp.arange(slot_count, dtype=jnp.int32)
        sort_keys = jnp.where(slot_ids // CAP == hot_owner, slot_ids % CAP - CAP, placing)
        chosen = jnp.argsort(sort_keys)[:OV]
        owner_ids = chosen // CAP
        source_ids = jax.random.permutation(source_key, NBLK)[:OV]
        target_ids = jax.random.randint(target_key, (OV,), 0, NBLK)
        listing = jnp.stack([source_ids, owner_ids, target_ids], 1)
        return listing[jax.random.permutation(order_key, OV)]

    def one_section(section_key):
        hot_owner = jax.random.randint(jax.random.fold_in(section_key, 1), (), 0, OWNERS)
        band_keys = jax.random.split(jax.random.fold_in(section_key, 2), OWNERS)
        return jax.vmap(one_band, in_axes=(0, None))(band_keys, hot_owner)
    section_keys = jax.random.split(jax.random.fold_in(key, 31), SECTIONS)
    return jax.vmap(one_section)(section_keys).astype(jnp.int32)


def with_ends(result, own_key, smallest, high):
    shape = result.shape
    index_at = [jax.random.randint(jax.random.fold_in(own_key, axis), (), 0, shape[axis]) for axis in range(len(shape))]
    result = result.at[tuple(index_at)].set(smallest)
    longest = shape.index(max(shape))
    index_at[longest] = (index_at[longest] + 1) % shape[longest]
    return result.at[tuple(index_at)].set(high)


def block_levels(stream_key, extent, cuts, smallest, top_value):
    loudness, own = 1.0, jax.random.fold_in(stream_key, 6)
    for axis_at, shards_of in cuts:
        heights = jnp.exp(jax.random.uniform(jax.random.fold_in(own, axis_at), (shards_of,), jnp.float32, smallest / len(cuts), top_value / len(cuts)))
        loudness = loudness * jnp.repeat(heights, extent[axis_at] // shards_of).reshape([-1 if axis == axis_at else 1 for axis in range(len(extent))])
    return loudness


def setup_inputs(seed: int = 0, part: int = 0) -> dict:
    keys = jax.random.split(jax.random.key(seed), 6)
    part_keys = jax.random.split(jax.random.fold_in(keys[5], part), 6)
    section_pixels = draw_section_pixels(jax.random.fold_in(jax.random.fold_in(keys[5], part), 71), part)
    jitter_index = draw_jitter_index(jax.random.fold_in(jax.random.fold_in(keys[5], part), 71), part)
    drift_list = draw_drift_list(jax.random.fold_in(jax.random.fold_in(keys[5], part), 71), part)
    blend_weight = jnp.clip(jnp.exp(math.log(2.0) - 1.3862944 * jax.random.uniform(part_keys[3], (SECTIONS, OWNERS, OV), jnp.float32) ** block_levels(part_keys[3], (SECTIONS, OWNERS, OV), ((0, 4),), -0.2, 0.2)), 0.5, 2.0)
    patch_col = with_ends(jax.random.randint(part_keys[4], (OWNERS, N_SEC), 0, W // N_SEC - PATCH + 1), jax.random.fold_in(part_keys[4], 1), 0, (W // N_SEC - PATCH + 1) - 1).astype(jnp.int32)
    return {"section_pixels": section_pixels, "jitter_index": jitter_index, "drift_list": drift_list, "blend_weight": blend_weight, "patch_col": patch_col}


def dft_tables(length):
    indices = jnp.arange(length, dtype=jnp.int32)
    products = indices[:, None] * indices[None, :] % length
    angles = products.astype(jnp.float32) * (2.0 * math.pi / length)
    return (jnp.cos(angles), jnp.sin(angles))

def align_rows(pixels, delays):
    row_width = pixels.shape[1]
    padded = jnp.pad(pixels, ((0, 0), (0, JMAX)))
    aligned = jnp.zeros_like(pixels)
    for shift_by in range(JMAX):
        aligned = aligned + jnp.where(delays[:, None] == shift_by, padded[:, shift_by:shift_by + row_width], 0.0)
    return aligned

def row_spectra(rows):
    row_count, row_width = rows.shape
    cosine_table, sine_table = dft_tables(SEG)
    dft_table = jnp.concatenate([cosine_table, -sine_table], 1)
    spectra = jnp.dot(rows.reshape(row_count * (row_width // SEG), SEG), dft_table, precision=lax.Precision.HIGHEST, preferred_element_type=jnp.float32)
    spectra = spectra.reshape(row_count, row_width // SEG, 2 * SEG)
    return (spectra[..., :SEG], spectra[..., SEG:])

def jitter_estimate(now_real, now_imag, before_real, before_imag):
    indices = jnp.arange(SEG, dtype=jnp.int32)
    weights = jnp.sin(indices.astype(jnp.float32) * (2.0 * math.pi / SEG))
    cross_term = now_imag * before_real - now_real * before_imag
    numerator = lax.optimization_barrier(jnp.mean(weights * cross_term, axis=(1, 2)))
    power_sum = 0.5 * (now_real * now_real + now_imag * now_imag + before_real * before_real + before_imag * before_imag)
    return numerator / (lax.optimization_barrier(jnp.mean(power_sum, axis=(1, 2))) + 1e-05)

def correct_rows(aligned, jitter):
    padded = jnp.pad(aligned, ((0, 0), (1, 1)))
    slopes = 0.5 * (padded[:, 2:] - padded[:, :-2])
    return (aligned - jitter[:, None] * slopes).astype(jnp.bfloat16)

def left_mul(matrix, batch):
    return jnp.einsum('ij,...jk->...ik', matrix, batch, precision=lax.Precision.HIGHEST)

def right_mul(batch, matrix):
    return jnp.einsum('...ij,jk->...ik', batch, matrix, precision=lax.Precision.HIGHEST)

def correlate(patches):
    side = patches.shape[-1]
    cosine_table, sine_table = dft_tables(side)
    values = patches.astype(jnp.float32)
    first_cos = right_mul(values, cosine_table)
    first_sin = right_mul(values, sine_table)
    freq_real = left_mul(cosine_table, first_cos) - left_mul(sine_table, first_sin)
    freq_imag = -(left_mul(sine_table, first_cos) + left_mul(cosine_table, first_sin))
    cross_real = freq_real[:-1] * freq_real[1:] + freq_imag[:-1] * freq_imag[1:]
    cross_imag = freq_imag[:-1] * freq_real[1:] - freq_real[:-1] * freq_imag[1:]
    magnitude = jnp.sqrt(cross_real * cross_real + cross_imag * cross_imag)
    damping = 0.5 * lax.optimization_barrier(jnp.mean(magnitude, axis=(-2, -1), keepdims=True)) + 1e-06
    scaled = 1.0 / (magnitude + damping)
    damped_real = cross_real * scaled
    damped_imag = cross_imag * scaled
    back_real = right_mul(damped_real, cosine_table) - right_mul(damped_imag, sine_table)
    back_imag = right_mul(damped_real, sine_table) + right_mul(damped_imag, cosine_table)
    return (left_mul(cosine_table, back_real) - left_mul(sine_table, back_imag)) / side

def prepare(inputs):
    pixels, delays = inputs
    aligned = align_rows(pixels, delays)
    now_real, now_imag = row_spectra(aligned)
    zero_row = jnp.zeros_like(now_real[:1])
    before_real = jnp.concatenate([zero_row, now_real[:-1]], 0)
    before_imag = jnp.concatenate([zero_row, now_imag[:-1]], 0)
    jitter = jitter_estimate(now_real, now_imag, before_real, before_imag)
    return (correct_rows(aligned, jitter), jitter)

def blend_section(inputs):
    corrected, drifts, weights = inputs
    band_rows = ROWS_DEV // BLOCK
    across = W // BLOCK
    blocks = corrected.reshape(OWNERS, band_rows, BLOCK, across, BLOCK).transpose(0, 1, 3, 2, 4)
    blocks = blocks.reshape(OWNERS * NBLK, BLOCK, BLOCK).astype(jnp.float32)
    source_index = (jnp.arange(OWNERS, dtype=jnp.int32)[:, None] * NBLK + drifts[:, :, 0]).reshape(-1)
    target_index = (drifts[:, :, 1] * NBLK + drifts[:, :, 2]).reshape(-1)
    mixing = (jnp.arange(OWNERS * NBLK, dtype=jnp.int32)[:, None] == target_index[None, :]).astype(jnp.float32)
    mixing = mixing * weights.reshape(-1)[None, :]
    incoming = jnp.einsum('nm,mxy->nxy', mixing, blocks[source_index], precision=lax.Precision.HIGHEST)
    merged = (blocks + incoming) / (1.0 + lax.optimization_barrier(jnp.sum(mixing, axis=1)))[:, None, None]
    merged = merged.reshape(OWNERS, band_rows, across, BLOCK, BLOCK).transpose(0, 1, 3, 2, 4)
    return merged.reshape(ROWS, W).astype(jnp.bfloat16)

def reference(section_pixels, jitter_index, drift_list, blend_weight, patch_col):
    corrected, jitter = lax.map(prepare, (section_pixels, jitter_index))
    montage = lax.map(blend_section, (corrected, drift_list, blend_weight))
    slab_width = W // N_SEC
    patch_rows = ROWS_DEV // PATCH
    bands = montage.reshape(SECTIONS, ROWS // PATCH, PATCH, W)

    def slab_surfaces(slab_index):
        starts = slab_index * slab_width + jnp.repeat(patch_col[:, slab_index], patch_rows)
        picked = jax.vmap(lambda one_band, start_col: lax.dynamic_slice_in_dim(one_band, start_col, PATCH, 2), in_axes=(1, 0), out_axes=1)(bands, starts)
        return correlate(picked)
    surfaces = lax.map(slab_surfaces, jnp.arange(N_SEC, dtype=jnp.int32))
    return (jitter, jnp.transpose(surfaces, (1, 2, 0, 3, 4)))
```

```python
import functools
import math

import jax
import jax.numpy as jnp
import numpy as np
from jax import lax
from jax.experimental import pallas as pl
from jax.experimental.pallas import tpu as pltpu
from jax.sharding import PartitionSpec as P

SEG = 512
PATCH = 128
BLOCK = 128
JMAX = 8
CAP = 2
LANES = 128
MESH = pl.DeviceIdType.MESH


def dft_tables(side):
    index = np.arange(side)
    angles = (index[:, None] * index[None, :] % side) * (2.0 * math.pi / side)
    cosine, sine = np.cos(angles), np.sin(angles)
    table = np.concatenate(
        [
            np.concatenate([cosine, sine], 1),
            np.concatenate([cosine, -sine], 1),
            np.concatenate([-sine, -cosine], 1),
        ],
        0,
    )
    high = table.astype(jnp.bfloat16)
    low = (table - high.astype(np.float64)).astype(jnp.bfloat16)
    return np.stack([high, low])


def dot(a, b):
    return jnp.dot(a, b, preferred_element_type=jnp.float32)


def split(a):
    high = a.astype(jnp.bfloat16)
    return high, (a - high.astype(jnp.float32)).astype(jnp.bfloat16)


def dot3(a, b):
    return dot(a[0], b[0]) + (dot(a[0], b[1]) + dot(a[1], b[0]))


def kernel(
    sizes,
    pixels,
    delays,
    drifts,
    weights,
    columns,
    tables_hbm,
    jitter_out,
    surfaces_out,
    raw,
    tables,
    delay_rows,
    aligned,
    slopes,
    cross_sums,
    energies,
    jitter_rows,
    halo_out,
    halo_in,
    outbox,
    arrived,
    patch_out,
    patch_in,
    freq,
    load_sem,
    table_sem,
    halo_send,
    halo_recv,
    block_send,
    block_recv,
    patch_send,
    patch_recv,
):
    sections, tiles, rows_axis, row_count, row_width, moves, chunks = sizes
    owners = tiles * rows_axis
    blocks = row_width // LANES
    groups = row_count // 8
    chunk_rows = row_count // chunks
    per_seg = SEG // LANES
    me = lax.axis_index("tile") * rows_axis + lax.axis_index("row")
    section = lax.axis_index("sec")

    def band_device(band):
        return {"tile": band // rows_axis, "row": band % rows_axis}

    table_copy = pltpu.make_async_copy(tables_hbm, tables, table_sem)
    loads = [
        pltpu.make_async_copy(
            pixels.at[0, pl.ds(c * chunk_rows, chunk_rows)],
            raw.at[pl.ds(c * chunk_rows, chunk_rows)],
            load_sem.at[c],
        )
        for c in range(chunks)
    ]
    loads[chunks - 1].start()
    for c in range(chunks - 1):
        loads[c].start()
    table_copy.start()

    barrier = pltpu.get_barrier_semaphore()
    for step in range(1, owners):
        pl.semaphore_signal(
            barrier, inc=1, device_id=band_device((me + step) % owners), device_id_type=MESH
        )
    for step in range(1, sections):
        pl.semaphore_signal(
            barrier, inc=1, device_id={"sec": (section + step) % sections}, device_id_type=MESH
        )

    lane = lax.broadcasted_iota(jnp.int32, (8, LANES), 1)
    first_lane, last_lane = lane == 0, lane == LANES - 1
    delay_rows[...] = jnp.broadcast_to(
        delays[...].astype(jnp.float32), (LANES, row_count)
    ).T
    zero = jnp.zeros((8, LANES), jnp.float32)
    for block in range(blocks):
        aligned[block, 0:8, :] = zero

    def align(start):
        delay = delay_rows[pl.ds(start, 8), :].astype(jnp.int32)
        values = [raw[pl.ds(start, 8), v * LANES : (v + 1) * LANES] for v in range(blocks)]
        distance = JMAX // 2
        while distance:
            chosen = (delay & distance) != 0
            kept = lane < LANES - distance
            turned = [pltpu.roll(x, LANES - distance, 1) for x in values] + [zero]
            values = [
                jnp.where(chosen, jnp.where(kept, turned[v], turned[v + 1]), values[v])
                for v in range(blocks)
            ]
            distance //= 2
        return values

    def differences(values):
        before = [pltpu.roll(x, 1, 1) for x in values]
        after = [pltpu.roll(x, LANES - 1, 1) for x in values]
        line, ring = [], []
        for v in range(blocks):
            left = jnp.where(first_lane, before[v - 1] if v else zero, before[v])
            right = jnp.where(last_lane, after[v + 1] if v < blocks - 1 else zero, after[v])
            line.append(right - left)
            if v % per_seg == 0:
                left = jnp.where(first_lane, before[v + per_seg - 1], before[v])
            if v % per_seg == per_seg - 1:
                right = jnp.where(last_lane, after[v - per_seg + 1], after[v])
            ring.append(right - left)
        return line, ring

    def total(terms):
        terms = list(terms)
        while len(terms) > 1:
            terms = [
                terms[i] + terms[i + 1] if i + 1 < len(terms) else terms[i]
                for i in range(0, len(terms), 2)
            ]
        return terms[0]

    loads[chunks - 1].wait()
    last = align(row_count - 8)
    for v in range(blocks):
        halo_out[v, :, :] = last[v]
    pl.semaphore_wait(barrier, owners + sections - 2)
    halo = pltpu.make_async_remote_copy(
        src_ref=halo_out.at[:, pl.ds(7, 1)],
        dst_ref=halo_in,
        send_sem=halo_send,
        recv_sem=halo_recv,
        device_id=band_device((me + 1) % owners),
        device_id_type=MESH,
    )
    halo.start()

    def group_step(g, carry):
        start = pl.multiple_of(g * 8, 8)
        values = align(start)
        for v in range(blocks):
            aligned[v, pl.ds(start + 8, 8), :] = values[v]
        line, ring = differences(values)
        for v in range(blocks):
            slopes[v, pl.ds(start, 8), :] = 0.5 * line[v]
        energies[pl.ds(start + 8, 8), :] = total(x * x for x in values)
        cross_sums[pl.ds(start, 8), :] = total(
            aligned[v, pl.ds(start + 7, 8), :] * ring[v] for v in range(blocks)
        )
        return carry

    per_chunk = groups // chunks
    for c in range(chunks):
        if c < chunks - 1:
            loads[c].wait()
        lax.fori_loop(c * per_chunk, (c + 1) * per_chunk, group_step, 0)

    def find(band, owner, rank):
        source, target, weight = jnp.int32(0), jnp.int32(-1), jnp.float32(0.0)
        seen = jnp.int32(0)
        for k in range(moves):
            hit = drifts[0, band, k, 1] == owner
            here = hit & (seen == rank)
            source = jnp.where(here, drifts[0, band, k, 0], source)
            target = jnp.where(here, drifts[0, band, k, 2], target)
            weight = jnp.where(here, weights[0, band, k], weight)
            seen = seen + hit.astype(jnp.int32)
        return source, target, weight

    _, ring0 = differences([aligned[v, 8:16, :] for v in range(blocks)])
    halo.wait_recv()
    is_first = me == 0
    above = [
        jnp.where(is_first, 0.0, jnp.broadcast_to(halo_in[v], (8, LANES))) for v in range(blocks)
    ]
    row = lax.broadcasted_iota(jnp.int32, (8, LANES), 0)
    cross_sums[0:8, :] = jnp.where(
        row == 0, total(above[v] * ring0[v] for v in range(blocks)), cross_sums[0:8, :]
    )
    energies[0:8, :] = total(a * a for a in above)
    segs = row_width // SEG
    numerator = jnp.sum(cross_sums[...], axis=1, keepdims=True) * (-0.5 / segs)
    power = jnp.sum(
        energies[8 : 8 + row_count, :] + energies[7 : 7 + row_count, :], axis=1, keepdims=True
    ) * (0.5 / segs)
    jitter_rows[...] = jnp.broadcast_to(numerator / (power + 1e-05), (row_count, LANES))
    jitter_out[...] = jitter_rows[...].T[0:1, :]

    def corrected(block):
        return (
            aligned[block, 8 : 8 + row_count, :] - jitter_rows[...] * slopes[block]
        ).astype(jnp.bfloat16)

    block_copies = []
    for step in range(owners - 1, -1, -1):
        owner = (me + step) % owners
        for rank in range(CAP):
            source, _, _ = find(me, owner, rank)
            value = corrected(source)
            if step:
                outbox[step, rank] = value
            else:
                arrived[me, rank] = value
        if step:
            copy = pltpu.make_async_remote_copy(
                src_ref=outbox.at[step],
                dst_ref=arrived.at[me],
                send_sem=block_send.at[step],
                recv_sem=block_recv.at[step],
                device_id=band_device(owner),
                device_id_type=MESH,
            )
            copy.start()
            block_copies.append(copy)

    incoming = []
    for band in range(owners):
        for rank in range(CAP):
            _, target, weight = find(band, me, rank)
            incoming.append((band, rank, target, weight))
    for copy in block_copies:
        copy.wait_recv()

    def merged(block):
        value = corrected(block).astype(jnp.float32)
        norm = jnp.float32(1.0)
        for band, rank, target, weight in incoming:
            share = jnp.where(target == block, weight, 0.0)
            value = value + share * arrived[band, rank].astype(jnp.float32)
            norm = norm + share
        return (value / jnp.full((row_count, LANES), norm)).astype(jnp.bfloat16)

    slab_blocks = blocks // sections
    place = lax.broadcasted_iota(jnp.int32, (2 * LANES, LANES), 0) - lax.broadcasted_iota(
        jnp.int32, (2 * LANES, LANES), 1
    )
    patch_copies = []
    for step in list(range(1, sections)) + [0]:
        slab = (section + step) % sections
        offset = columns[0, slab]
        block = slab * slab_blocks + offset // LANES
        pair = jnp.concatenate([merged(block), merged(jnp.minimum(block + 1, blocks - 1))], 1)
        pick = (place == offset % LANES).astype(jnp.float32).astype(jnp.bfloat16)
        patch = dot(pair, pick).astype(jnp.bfloat16)
        if step:
            patch_out[step] = patch
            copy = pltpu.make_async_remote_copy(
                src_ref=patch_out.at[step],
                dst_ref=patch_in.at[section],
                send_sem=patch_send.at[step],
                recv_sem=patch_recv.at[step],
                device_id={"sec": slab},
                device_id_type=MESH,
            )
            copy.start()
            patch_copies.append(copy)
        else:
            patch_in[section] = patch

    table_copy.wait()
    wide = tables[0, 0:PATCH, :], tables[1, 0:PATCH, :]
    square = tables[0, PATCH : 3 * PATCH, :], tables[1, PATCH : 3 * PATCH, :]
    for step in range(sections):
        if step:
            patch_copies[step - 1].wait_recv()
        source = (section - step + sections) % sections
        patch = patch_in[source]
        first = dot(patch, wide[0]) + dot(patch, wide[1])
        stacked = jnp.concatenate([first[:, :PATCH], first[:, PATCH:]], 0)
        freq[source] = dot3(square, split(stacked))
    for s in range(sections - 1):
        now_real, now_imag = freq[s, 0:PATCH], freq[s, PATCH : 2 * PATCH]
        next_real, next_imag = freq[s + 1, 0:PATCH], freq[s + 1, PATCH : 2 * PATCH]
        cross_real = now_real * next_real + now_imag * next_imag
        cross_imag = now_imag * next_real - now_real * next_imag
        magnitude = jnp.sqrt(cross_real * cross_real + cross_imag * cross_imag)
        mean = jnp.sum(jnp.sum(magnitude, axis=0, keepdims=True), axis=1, keepdims=True) * (
            1.0 / (PATCH * PATCH)
        )
        scaled = 1.0 / (magnitude + (0.5 * mean + 1e-06))
        damped = jnp.concatenate([cross_real * scaled, cross_imag * scaled], 1)
        back = dot3(split(damped), square)
        stacked = jnp.concatenate([back[:, :PATCH], back[:, PATCH:]], 0)
        surfaces_out[s, 0, 0] = dot3(wide, split(stacked)) * (1.0 / PATCH)

    halo.wait_send()
    for copy in block_copies + patch_copies:
        copy.wait_send()


def per_device(section_pixels, jitter_index, drift_list, blend_weight, patch_col):
    _, row_count, row_width = section_pixels.shape
    sections = lax.axis_size("sec")
    tiles, rows_axis = lax.axis_size("tile"), lax.axis_size("row")
    owners = tiles * rows_axis
    moves = drift_list.shape[2]
    blocks = row_width // LANES
    chunks = 4
    sizes = (sections, tiles, rows_axis, row_count, row_width, moves, chunks)
    tables = jnp.asarray(dft_tables(PATCH))
    f32, bf16 = jnp.float32, jnp.bfloat16
    vmem = pl.BlockSpec(memory_space=pltpu.VMEM)
    smem = pl.BlockSpec(memory_space=pltpu.SMEM)
    anywhere = pl.BlockSpec(memory_space=pl.ANY)
    dma = pltpu.SemaphoreType.DMA
    return pl.pallas_call(
        functools.partial(kernel, sizes),
        out_shape=(
            jax.ShapeDtypeStruct((1, row_count), f32),
            jax.ShapeDtypeStruct((sections - 1, 1, 1, PATCH, PATCH), f32),
        ),
        in_specs=[anywhere, vmem, smem, smem, smem, anywhere],
        out_specs=(vmem, vmem),
        scratch_shapes=[
            pltpu.VMEM((row_count, row_width), f32),
            pltpu.VMEM(tables.shape, bf16),
            pltpu.VMEM((row_count, LANES), f32),
            pltpu.VMEM((blocks, row_count + 8, LANES), f32),
            pltpu.VMEM((blocks, row_count, LANES), f32),
            pltpu.VMEM((row_count, LANES), f32),
            pltpu.VMEM((row_count + 8, LANES), f32),
            pltpu.VMEM((row_count, LANES), f32),
            pltpu.VMEM((blocks, 8, LANES), f32),
            pltpu.VMEM((blocks, 1, LANES), f32),
            pltpu.VMEM((owners, CAP, BLOCK, BLOCK), bf16),
            pltpu.VMEM((owners, CAP, BLOCK, BLOCK), bf16),
            pltpu.VMEM((sections, PATCH, PATCH), bf16),
            pltpu.VMEM((sections, PATCH, PATCH), bf16),
            pltpu.VMEM((sections, 2 * PATCH, PATCH), f32),
            dma((chunks,)),
            dma,
            dma,
            dma,
            dma((owners,)),
            dma((owners,)),
            dma((sections,)),
            dma((sections,)),
        ],
        compiler_params=pltpu.CompilerParams(collective_id=0, has_side_effects=True),
        name="section_correlation",
    )(section_pixels, jitter_index, drift_list, blend_weight, patch_col, tables)


def solution(mesh):
    in_specs = (
        P(("groups", "sec"), ("tile", "row"), None),
        P(("groups", "sec"), ("tile", "row")),
        P(("groups", "sec"), None, None, None),
        P(("groups", "sec"), None, None),
        P(("tile", "row"), "groups"),
    )
    out_specs = (
        P(("groups", "sec"), ("tile", "row")),
        P("groups", ("tile", "row"), "sec", None, None),
    )
    return jax.shard_map(
        per_device, mesh=mesh, in_specs=in_specs, out_specs=out_specs, check_vma=False
    )
```

```python
import functools
import math

import jax
import jax.numpy as jnp
import numpy as np
from jax import lax
from jax.experimental import pallas as pl
from jax.experimental.pallas import tpu as pltpu
from jax.sharding import PartitionSpec as P

SEG = 512
PATCH = 128
BLOCK = 128
CAP = 2
LANES = 128
MESH = pl.DeviceIdType.MESH


def dft_tables(side):
    index = np.arange(side)
    angles = (index[:, None] * index[None, :] % side) * (2.0 * math.pi / side)
    cosine, sine = np.cos(angles), np.sin(angles)
    table = np.concatenate(
        [
            np.concatenate([cosine, sine], 1),
            np.concatenate([cosine, -sine], 1),
            np.concatenate([-sine, -cosine], 1),
        ],
        0,
    )
    high = table.astype(jnp.bfloat16)
    low = (table - high.astype(np.float64)).astype(jnp.bfloat16)
    return np.stack([high, low])


def dot(a, b):
    return jnp.dot(a, b, preferred_element_type=jnp.float32)


def split(a):
    high = a.astype(jnp.bfloat16)
    return high, (a - high.astype(jnp.float32)).astype(jnp.bfloat16)


def dot3(a, b):
    return dot(a[0], b[0]) + (dot(a[0], b[1]) + dot(a[1], b[0]))


def kernel(
    sizes,
    pixels,
    delays_hbm,
    drifts_hbm,
    weights_hbm,
    columns_hbm,
    tables_hbm,
    jitter_out,
    freq,
    raw,
    tables,
    delays,
    drifts,
    weights,
    columns,
    delay_rows,
    aligned,
    slopes,
    cross_sums,
    energies,
    jitter_rows,
    halo_out,
    halo_in,
    outbox,
    arrived,
    blend,
    patch_out,
    patch_in,
    load_sem,
    table_sem,
    small_sem,
    halo_send,
    halo_recv,
    block_send,
    block_recv,
    patch_send,
    patch_recv,
):
    sections, tiles, rows_axis, row_count, row_width, moves, chunks = sizes
    owners = tiles * rows_axis
    blocks = row_width // LANES
    groups = row_count // 8
    chunk_rows = row_count // chunks
    per_seg = SEG // LANES
    tile, row_at = lax.axis_index("tile"), lax.axis_index("row")
    me = tile * rows_axis + row_at
    section = lax.axis_index("sec")

    def band_device(band):
        return {"tile": band // rows_axis, "row": band % rows_axis}

    band_steps = [(t, r) for t in range(tiles) for r in range(rows_axis)][1:]
    band_steps.sort(key=lambda step: -min(step[0], tiles - step[0]))

    def band_at(step):
        return (tile + step[0]) % tiles * rows_axis + (row_at + step[1]) % rows_axis

    def band_from(step):
        return (tile - step[0] + tiles) % tiles * rows_axis + (
            row_at - step[1] + rows_axis
        ) % rows_axis

    section_steps = sorted(range(1, sections), key=lambda step: -min(step, sections - step))

    table_copy = pltpu.make_async_copy(tables_hbm, tables, table_sem)
    loads = [
        pltpu.make_async_copy(
            pixels.at[0, pl.ds(c * chunk_rows, chunk_rows)],
            raw.at[pl.ds(c * chunk_rows, chunk_rows)],
            load_sem.at[c],
        )
        for c in range(chunks)
    ]
    small_copies = [
        pltpu.make_async_copy(source, target, small_sem.at[i])
        for i, (source, target) in enumerate(
            (
                (delays_hbm, delays),
                (drifts_hbm, drifts),
                (weights_hbm, weights),
                (columns_hbm, columns),
            )
        )
    ]
    small_copies[0].start()
    loads[chunks - 1].start()
    for c in range(chunks - 1):
        loads[c].start()
    for copy in small_copies[1:]:
        copy.start()
    table_copy.start()

    barrier = pltpu.get_barrier_semaphore()
    for step in range(1, owners):
        pl.semaphore_signal(
            barrier, inc=1, device_id=band_device((me + step) % owners), device_id_type=MESH
        )
    for step in range(1, sections):
        pl.semaphore_signal(
            barrier, inc=1, device_id={"sec": (section + step) % sections}, device_id_type=MESH
        )

    lane = lax.broadcasted_iota(jnp.int32, (8, LANES), 1)
    first_lane, last_lane = lane == 0, lane == LANES - 1
    small_copies[0].wait()
    delay_rows[...] = jnp.broadcast_to(
        delays[...].astype(jnp.float32), (LANES, row_count)
    ).T
    zero = jnp.zeros((8, LANES), jnp.float32)
    for block in range(blocks):
        aligned[block, 0:8, :] = zero

    def align(start):
        delay = delay_rows[pl.ds(start, 8), :].astype(jnp.int32)
        values = [raw[pl.ds(start, 8), v * LANES : (v + 1) * LANES] for v in range(blocks)]
        index = lane + delay
        kept = index < LANES
        index = index & (LANES - 1)
        turned = [jnp.take_along_axis(x, index, axis=1) for x in values] + [zero]
        values = [jnp.where(kept, turned[v], turned[v + 1]) for v in range(blocks)]
        return values

    def differences(values):
        before = [pltpu.roll(x, 1, 1) for x in values]
        after = [pltpu.roll(x, LANES - 1, 1) for x in values]
        line, ring = [], []
        for v in range(blocks):
            left = jnp.where(first_lane, before[v - 1] if v else zero, before[v])
            right = jnp.where(last_lane, after[v + 1] if v < blocks - 1 else zero, after[v])
            line.append(right - left)
            if v % per_seg == 0:
                left = jnp.where(first_lane, before[v + per_seg - 1], before[v])
            if v % per_seg == per_seg - 1:
                right = jnp.where(last_lane, after[v - per_seg + 1], after[v])
            ring.append(right - left)
        return line, ring

    def total(terms):
        terms = list(terms)
        while len(terms) > 1:
            terms = [
                terms[i] + terms[i + 1] if i + 1 < len(terms) else terms[i]
                for i in range(0, len(terms), 2)
            ]
        return terms[0]

    loads[chunks - 1].wait()
    last = align(row_count - 8)
    for v in range(blocks):
        halo_out[v, :, :] = last[v]
    pl.semaphore_wait(barrier, owners + sections - 2)
    halo = pltpu.make_async_remote_copy(
        src_ref=halo_out.at[:, pl.ds(7, 1)],
        dst_ref=halo_in,
        send_sem=halo_send,
        recv_sem=halo_recv,
        device_id=band_device((me + 1) % owners),
        device_id_type=MESH,
    )
    halo.start()

    def group_step(g, carry):
        start = pl.multiple_of(g * 8, 8)
        values = align(start)
        for v in range(blocks):
            aligned[v, pl.ds(start + 8, 8), :] = values[v]
        line, ring = differences(values)
        for v in range(blocks):
            slopes[v, pl.ds(start, 8), :] = 0.5 * line[v]
        energies[pl.ds(start + 8, 8), :] = total(x * x for x in values)
        cross_sums[pl.ds(start, 8), :] = total(
            aligned[v, pl.ds(start + 7, 8), :] * ring[v] for v in range(blocks)
        )
        return carry

    per_chunk = groups // chunks
    for c in range(chunks):
        if c < chunks - 1:
            loads[c].wait()
        lax.fori_loop(c * per_chunk, (c + 1) * per_chunk, group_step, 0)

    def find(band, owner, rank):
        source, target, weight = jnp.int32(0), jnp.int32(-1), jnp.float32(0.0)
        seen = jnp.int32(0)
        for k in range(moves):
            hit = drifts[0, 1, band, k] == owner
            here = hit & (seen == rank)
            source = jnp.where(here, drifts[0, 0, band, k], source)
            target = jnp.where(here, drifts[0, 2, band, k], target)
            weight = jnp.where(here, weights[0, band, k], weight)
            seen = seen + hit.astype(jnp.int32)
        return source, target, weight

    for copy in small_copies[1:]:
        copy.wait()
    sources = {}
    for step in band_steps + [(0, 0)]:
        for rank in range(CAP):
            sources[step, rank] = find(me, band_at(step), rank)[0]

    _, ring0 = differences([aligned[v, 8:16, :] for v in range(blocks)])
    halo.wait_recv()
    is_first = me == 0
    above = [
        jnp.where(is_first, 0.0, jnp.broadcast_to(halo_in[v], (8, LANES))) for v in range(blocks)
    ]
    row = lax.broadcasted_iota(jnp.int32, (8, LANES), 0)
    cross_sums[0:8, :] = jnp.where(
        row == 0, total(above[v] * ring0[v] for v in range(blocks)), cross_sums[0:8, :]
    )
    energies[0:8, :] = total(a * a for a in above)
    segs = row_width // SEG
    numerator = jnp.sum(cross_sums[...], axis=1, keepdims=True) * (-0.5 / segs)
    power = jnp.sum(
        energies[8 : 8 + row_count, :] + energies[7 : 7 + row_count, :], axis=1, keepdims=True
    ) * (0.5 / segs)
    jitter_rows[...] = jnp.broadcast_to(numerator / (power + 1e-05), (row_count, LANES))
    jitter_out[...] = jitter_rows[...].T[0:1, :]

    def corrected(block):
        return (
            aligned[block, 8 : 8 + row_count, :] - jitter_rows[...] * slopes[block]
        ).astype(jnp.bfloat16)

    block_copies = {}
    for step in band_steps:
        slot = step[0] * rows_axis + step[1]
        for rank in range(CAP):
            outbox[slot, rank] = corrected(sources[step, rank])
        copy = pltpu.make_async_remote_copy(
            src_ref=outbox.at[slot],
            dst_ref=arrived.at[slot],
            send_sem=block_send.at[slot],
            recv_sem=block_recv.at[slot],
            device_id=band_device(band_at(step)),
            device_id_type=MESH,
        )
        copy.start()
        block_copies[step] = copy

    slab_blocks = blocks // sections
    slabs = [(section + step) % sections for step in range(sections)]
    offsets = [columns[0, slab] for slab in slabs]
    under = []
    for step in range(sections):
        block = slabs[step] * slab_blocks + offsets[step] // LANES
        under += [block, jnp.minimum(block + 1, blocks - 1)]
    norms = [jnp.float32(1.0)] * len(under)
    shares = {}
    for step in [(0, 0)] + band_steps:
        for rank in range(CAP):
            _, target, weight = find(band_from(step), me, rank)
            shares[step, rank] = [jnp.where(target == block, weight, 0.0) for block in under]
            norms = [norm + share for norm, share in zip(norms, shares[step, rank])]
    own = [corrected(sources[(0, 0), rank]).astype(jnp.float32) for rank in range(CAP)]
    for i, block in enumerate(under):
        value = corrected(block).astype(jnp.float32)
        for rank in range(CAP):
            value = value + shares[(0, 0), rank][i] * own[rank]
        blend[i] = value

    def with_shares(step, i, value, rows):
        slot = step[0] * rows_axis + step[1]
        for rank in range(CAP):
            value = value + shares[step, rank][i] * arrived[slot, rank, rows, :].astype(jnp.float32)
        return value

    part = row_count // 4
    for step in band_steps[:0:-1]:
        block_copies[step].wait_recv()
        for p in range(4):
            rows = slice(p * part, (p + 1) * part)
            for i in range(len(under)):
                blend[i, rows, :] = with_shares(step, i, blend[i, rows, :], rows)
    last_step = band_steps[0]
    block_copies[last_step].wait_recv()

    def merged(i):
        value = with_shares(last_step, i, blend[i], slice(0, row_count))
        share = 1.0 / jnp.full((8, LANES), norms[i])
        return (value * share[0:1, :]).astype(jnp.bfloat16)

    place = lax.broadcasted_iota(jnp.int32, (2 * LANES, LANES), 0) - lax.broadcasted_iota(
        jnp.int32, (2 * LANES, LANES), 1
    )
    patch_copies = {}
    for step in section_steps + [0]:
        pair = jnp.concatenate([merged(2 * step), merged(2 * step + 1)], 1)
        pick = (place == offsets[step] % LANES).astype(jnp.float32).astype(jnp.bfloat16)
        patch = dot(pair, pick).astype(jnp.bfloat16)
        if step:
            patch_out[step] = patch
            copy = pltpu.make_async_remote_copy(
                src_ref=patch_out.at[step],
                dst_ref=patch_in.at[step],
                send_sem=patch_send.at[step],
                recv_sem=patch_recv.at[step],
                device_id={"sec": slabs[step]},
                device_id_type=MESH,
            )
            copy.start()
            patch_copies[step] = copy
        else:
            patch_in[0] = patch

    table_copy.wait()
    wide = tables[0, 0:PATCH, :], tables[1, 0:PATCH, :]
    square = tables[0, PATCH : 3 * PATCH, :], tables[1, PATCH : 3 * PATCH, :]
    for step in [0] + section_steps[::-1]:
        if step:
            patch_copies[step].wait_recv()
        source = (section - step + sections) % sections
        patch = patch_in[step]
        first = dot(patch, wide[0]) + dot(patch, wide[1])
        stacked = jnp.concatenate([first[:, :PATCH], first[:, PATCH:]], 0)
        freq[source] = dot3(square, split(stacked))

    halo.wait_send()
    for copy in list(block_copies.values()) + list(patch_copies.values()):
        copy.wait_send()


def correlate(freq, tables, jitter, jitter_out, surfaces_out):
    jitter_out[...] = jitter[...]
    wide = tables[0:PATCH, :]
    square = tables[PATCH : 3 * PATCH, :]
    for s in range(freq.shape[0] - 1):
        now_real, now_imag = freq[s, 0:PATCH], freq[s, PATCH : 2 * PATCH]
        next_real, next_imag = freq[s + 1, 0:PATCH], freq[s + 1, PATCH : 2 * PATCH]
        cross_real = now_real * next_real + now_imag * next_imag
        cross_imag = now_imag * next_real - now_real * next_imag
        magnitude = jnp.sqrt(cross_real * cross_real + cross_imag * cross_imag)
        mean = jnp.sum(jnp.sum(magnitude, axis=0, keepdims=True), axis=1, keepdims=True) * (
            1.0 / (PATCH * PATCH)
        )
        scaled = 1.0 / (magnitude + (0.5 * mean + 1e-06))
        damped = jnp.concatenate([cross_real * scaled, cross_imag * scaled], 1)
        back = dot(damped.astype(jnp.bfloat16), square)
        stacked = jnp.concatenate([back[:, :PATCH], back[:, PATCH:]], 0)
        surfaces_out[s, 0, 0] = dot(wide, stacked.astype(jnp.bfloat16)) * (1.0 / PATCH)


def per_device(section_pixels, jitter_index, drift_list, blend_weight, patch_col):
    _, row_count, row_width = section_pixels.shape
    sections = lax.axis_size("sec")
    tiles, rows_axis = lax.axis_size("tile"), lax.axis_size("row")
    owners = tiles * rows_axis
    moves = drift_list.shape[2]
    blocks = row_width // LANES
    chunks = 4
    sizes = (sections, tiles, rows_axis, row_count, row_width, moves, chunks)
    tables = dft_tables(PATCH)
    f32, bf16 = jnp.float32, jnp.bfloat16
    vmem = pl.BlockSpec(memory_space=pltpu.VMEM)
    anywhere = pl.BlockSpec(memory_space=pl.ANY)
    dma = pltpu.SemaphoreType.DMA
    jitter, freq = pl.pallas_call(
        functools.partial(kernel, sizes),
        out_shape=(
            jax.ShapeDtypeStruct((1, row_count), f32),
            jax.ShapeDtypeStruct((sections, 2 * PATCH, PATCH), f32),
        ),
        in_specs=[anywhere] * 6,
        out_specs=(vmem, vmem),
        scratch_shapes=[
            pltpu.VMEM((row_count, row_width), f32),
            pltpu.VMEM(tables.shape, bf16),
            pltpu.VMEM(jitter_index.shape, jnp.int32),
            pltpu.SMEM((1, 3, owners, moves), jnp.int32),
            pltpu.SMEM(blend_weight.shape, f32),
            pltpu.SMEM(patch_col.shape, jnp.int32),
            pltpu.VMEM((row_count, LANES), f32),
            pltpu.VMEM((blocks, row_count + 8, LANES), f32),
            pltpu.VMEM((blocks, row_count, LANES), f32),
            pltpu.VMEM((row_count, LANES), f32),
            pltpu.VMEM((row_count + 8, LANES), f32),
            pltpu.VMEM((row_count, LANES), f32),
            pltpu.VMEM((blocks, 8, LANES), f32),
            pltpu.VMEM((blocks, 1, LANES), f32),
            pltpu.VMEM((owners, CAP, BLOCK, BLOCK), bf16),
            pltpu.VMEM((owners, CAP, BLOCK, BLOCK), bf16),
            pltpu.VMEM((2 * sections, BLOCK, BLOCK), f32),
            pltpu.VMEM((sections, PATCH, PATCH), bf16),
            pltpu.VMEM((sections, PATCH, PATCH), bf16),
            dma((chunks,)),
            dma,
            dma((4,)),
            dma,
            dma,
            dma((owners,)),
            dma((owners,)),
            dma((sections,)),
            dma((sections,)),
        ],
        compiler_params=pltpu.CompilerParams(collective_id=0, has_side_effects=True),
        name="section_patches",
    )(
        section_pixels,
        jitter_index,
        jnp.transpose(drift_list, (0, 3, 1, 2)),
        blend_weight,
        patch_col,
        tables,
    )
    return pl.pallas_call(
        correlate,
        out_shape=(
            jax.ShapeDtypeStruct((1, row_count), f32),
            jax.ShapeDtypeStruct((sections - 1, 1, 1, PATCH, PATCH), f32),
        ),
        in_specs=[vmem] * 3,
        out_specs=(vmem, vmem),
        name="section_correlation",
    )(freq, tables[0], jitter)


def solution(mesh):
    in_specs = (
        P(("groups", "sec"), ("tile", "row"), None),
        P(("groups", "sec"), ("tile", "row")),
        P(("groups", "sec"), None, None, None),
        P(("groups", "sec"), None, None),
        P(("tile", "row"), "groups"),
    )
    out_specs = (
        P(("groups", "sec"), ("tile", "row")),
        P("groups", ("tile", "row"), "sec", None, None),
    )
    return jax.shard_map(
        per_device, mesh=mesh, in_specs=in_specs, out_specs=out_specs, check_vma=False
    )
```

```python
import functools
import math

import jax
import jax.numpy as jnp
import numpy as np
from jax import lax
from jax.experimental import pallas as pl
from jax.experimental.pallas import tpu as pltpu
from jax.sharding import PartitionSpec as P

SEG = 512
PATCH = 128
BLOCK = 128
CAP = 2
LANES = 128
MESH = pl.DeviceIdType.MESH


def dft_tables(side):
    index = np.arange(side)
    angles = (index[:, None] * index[None, :] % side) * (2.0 * math.pi / side)
    cosine, sine = np.cos(angles), np.sin(angles)
    table = np.concatenate(
        [
            np.concatenate([cosine, sine], 1),
            np.concatenate([cosine, -sine], 1),
            np.concatenate([-sine, -cosine], 1),
        ],
        0,
    )
    high = table.astype(jnp.bfloat16)
    low = (table - high.astype(np.float64)).astype(jnp.bfloat16)
    return np.stack([high, low])


def dot(a, b):
    return jnp.dot(a, b, preferred_element_type=jnp.float32)


def split(a):
    high = a.astype(jnp.bfloat16)
    return high, (a - high.astype(jnp.float32)).astype(jnp.bfloat16)


def dot3(a, b):
    return dot(a[0], b[0]) + (dot(a[0], b[1]) + dot(a[1], b[0]))


def kernel(
    sizes,
    pixels,
    delays_hbm,
    drifts_hbm,
    weights_hbm,
    columns_hbm,
    tables_hbm,
    jitter_out,
    freq,
    raw,
    tables,
    delays,
    drifts,
    weights,
    columns,
    delay_rows,
    aligned,
    slopes,
    cross_sums,
    energies,
    jitter_rows,
    halo_out,
    halo_in,
    outbox,
    arrived,
    patch_out,
    patch_in,
    load_sem,
    table_sem,
    small_sem,
    halo_send,
    halo_recv,
    block_send,
    block_recv,
    patch_send,
    patch_recv,
):
    sections, tiles, rows_axis, row_count, row_width, moves, chunks = sizes
    owners = tiles * rows_axis
    blocks = row_width // LANES
    groups = row_count // 8
    chunk_rows = row_count // chunks
    per_seg = SEG // LANES
    tile, row_at = lax.axis_index("tile"), lax.axis_index("row")
    me = tile * rows_axis + row_at
    section = lax.axis_index("sec")

    def band_device(band):
        return {"tile": band // rows_axis, "row": band % rows_axis}

    band_steps = [(t, r) for t in range(tiles) for r in range(rows_axis)][1:]
    band_steps.sort(key=lambda step: -min(step[0], tiles - step[0]))

    def band_at(step):
        return (tile + step[0]) % tiles * rows_axis + (row_at + step[1]) % rows_axis

    def band_from(step):
        return (tile - step[0] + tiles) % tiles * rows_axis + (
            row_at - step[1] + rows_axis
        ) % rows_axis

    section_steps = sorted(range(1, sections), key=lambda step: -min(step, sections - step))

    table_copy = pltpu.make_async_copy(tables_hbm, tables, table_sem)
    loads = [
        pltpu.make_async_copy(
            pixels.at[0, pl.ds(c * chunk_rows, chunk_rows)],
            raw.at[pl.ds(c * chunk_rows, chunk_rows)],
            load_sem.at[c],
        )
        for c in range(chunks)
    ]
    small_copies = [
        pltpu.make_async_copy(source, target, small_sem.at[i])
        for i, (source, target) in enumerate(
            (
                (delays_hbm, delays),
                (drifts_hbm, drifts),
                (weights_hbm, weights),
                (columns_hbm, columns),
            )
        )
    ]
    small_copies[0].start()
    loads[chunks - 1].start()
    for c in range(chunks - 1):
        loads[c].start()
    for copy in small_copies[1:]:
        copy.start()
    table_copy.start()

    barrier = pltpu.get_barrier_semaphore()
    for step in range(1, owners):
        pl.semaphore_signal(
            barrier, inc=1, device_id=band_device((me + step) % owners), device_id_type=MESH
        )
    for step in range(1, sections):
        pl.semaphore_signal(
            barrier, inc=1, device_id={"sec": (section + step) % sections}, device_id_type=MESH
        )

    lane = lax.broadcasted_iota(jnp.int32, (8, LANES), 1)
    first_lane, last_lane = lane == 0, lane == LANES - 1
    small_copies[0].wait()
    delay_rows[...] = jnp.broadcast_to(
        delays[...].astype(jnp.float32), (LANES, row_count)
    ).T
    zero = jnp.zeros((8, LANES), jnp.float32)
    for block in range(blocks):
        aligned[block, 0:8, :] = zero

    def align(start):
        delay = delay_rows[pl.ds(start, 8), :].astype(jnp.int32)
        values = [raw[pl.ds(start, 8), v * LANES : (v + 1) * LANES] for v in range(blocks)]
        index = lane + delay
        kept = index < LANES
        index = index & (LANES - 1)
        turned = [jnp.take_along_axis(x, index, axis=1) for x in values] + [zero]
        values = [jnp.where(kept, turned[v], turned[v + 1]) for v in range(blocks)]
        return values

    def differences(values):
        before = [pltpu.roll(x, 1, 1) for x in values]
        after = [pltpu.roll(x, LANES - 1, 1) for x in values]
        line, ring = [], []
        for v in range(blocks):
            left = jnp.where(first_lane, before[v - 1] if v else zero, before[v])
            right = jnp.where(last_lane, after[v + 1] if v < blocks - 1 else zero, after[v])
            line.append(right - left)
            if v % per_seg == 0:
                left = jnp.where(first_lane, before[v + per_seg - 1], before[v])
            if v % per_seg == per_seg - 1:
                right = jnp.where(last_lane, after[v - per_seg + 1], after[v])
            ring.append(right - left)
        return line, ring

    def total(terms):
        terms = list(terms)
        while len(terms) > 1:
            terms = [
                terms[i] + terms[i + 1] if i + 1 < len(terms) else terms[i]
                for i in range(0, len(terms), 2)
            ]
        return terms[0]

    loads[chunks - 1].wait()
    last = align(row_count - 8)
    for v in range(blocks):
        halo_out[v, :, :] = last[v]
    pl.semaphore_wait(barrier, owners + sections - 2)
    halo = pltpu.make_async_remote_copy(
        src_ref=halo_out.at[:, pl.ds(7, 1)],
        dst_ref=halo_in,
        send_sem=halo_send,
        recv_sem=halo_recv,
        device_id=band_device((me + 1) % owners),
        device_id_type=MESH,
    )
    halo.start()

    def group_step(g, carry):
        start = pl.multiple_of(g * 8, 8)
        values = align(start)
        for v in range(blocks):
            aligned[v, pl.ds(start + 8, 8), :] = values[v]
        line, ring = differences(values)
        for v in range(blocks):
            slopes[v, pl.ds(start, 8), :] = 0.5 * line[v]
        energies[pl.ds(start + 8, 8), :] = total(x * x for x in values)
        cross_sums[pl.ds(start, 8), :] = total(
            aligned[v, pl.ds(start + 7, 8), :] * ring[v] for v in range(blocks)
        )
        return carry

    def find(band, owner, rank):
        source, target, weight = jnp.int32(0), jnp.int32(-1), jnp.float32(0.0)
        seen = jnp.int32(0)
        for k in range(moves):
            hit = drifts[0, 1, band, k] == owner
            here = hit & (seen == rank)
            source = jnp.where(here, drifts[0, 0, band, k], source)
            target = jnp.where(here, drifts[0, 2, band, k], target)
            weight = jnp.where(here, weights[0, band, k], weight)
            seen = seen + hit.astype(jnp.int32)
        return source, target, weight

    for copy in small_copies[1:]:
        copy.wait()
    sources = {}
    for step in band_steps + [(0, 0)]:
        for rank in range(CAP):
            sources[step, rank] = find(me, band_at(step), rank)[0]

    segs = row_width // SEG

    def corrected(block, rows):
        shifted = slice(rows.start + 8, rows.stop + 8)
        return (
            aligned[block, shifted, :] - jitter_rows[rows, :] * slopes[block, rows, :]
        ).astype(jnp.bfloat16)

    block_copies = {}

    def finish_chunk(c):
        rows = slice(c * chunk_rows, (c + 1) * chunk_rows)
        numerator = jnp.sum(cross_sums[rows, :], axis=1, keepdims=True) * (-0.5 / segs)
        power = energies[rows.start + 8 : rows.stop + 8, :]
        power = power + energies[rows.start + 7 : rows.stop + 7, :]
        power = jnp.sum(power, axis=1, keepdims=True) * (0.5 / segs)
        jitter_rows[rows, :] = jnp.broadcast_to(numerator / (power + 1e-05), (chunk_rows, LANES))
        for step in band_steps:
            slot = step[0] * rows_axis + step[1]
            for rank in range(CAP):
                outbox[slot, rank, rows, :] = corrected(sources[step, rank], rows)
            copy = pltpu.make_async_remote_copy(
                src_ref=outbox.at[slot, :, pl.ds(rows.start, chunk_rows)],
                dst_ref=arrived.at[slot, :, pl.ds(rows.start, chunk_rows)],
                send_sem=block_send.at[slot, c],
                recv_sem=block_recv.at[slot, c],
                device_id=band_device(band_at(step)),
                device_id_type=MESH,
            )
            copy.start()
            block_copies[step, c] = copy

    per_chunk = groups // chunks
    for c in range(chunks):
        if c < chunks - 1:
            loads[c].wait()
        lax.fori_loop(c * per_chunk, (c + 1) * per_chunk, group_step, 0)
        if c:
            finish_chunk(c)

    _, ring0 = differences([aligned[v, 8:16, :] for v in range(blocks)])
    halo.wait_recv()
    is_first = me == 0
    above = [
        jnp.where(is_first, 0.0, jnp.broadcast_to(halo_in[v], (8, LANES))) for v in range(blocks)
    ]
    row = lax.broadcasted_iota(jnp.int32, (8, LANES), 0)
    cross_sums[0:8, :] = jnp.where(
        row == 0, total(above[v] * ring0[v] for v in range(blocks)), cross_sums[0:8, :]
    )
    energies[0:8, :] = total(a * a for a in above)
    finish_chunk(0)
    chunk_order = list(range(1, chunks)) + [0]

    slab_blocks = blocks // sections
    slabs = [(section + step) % sections for step in range(sections)]
    offsets = [columns[0, slab] for slab in slabs]
    under = []
    for step in range(sections):
        block = slabs[step] * slab_blocks + offsets[step] // LANES
        under += [block, jnp.minimum(block + 1, blocks - 1)]
    norms = [jnp.float32(1.0)] * len(under)
    shares = {}
    for step in [(0, 0)] + band_steps:
        for rank in range(CAP):
            _, target, weight = find(band_from(step), me, rank)
            shares[step, rank] = [jnp.where(target == block, weight, 0.0) for block in under]
            norms = [norm + share for norm, share in zip(norms, shares[step, rank])]
    lanes = lax.broadcasted_iota(jnp.int32, (chunk_rows, LANES), 1)
    patch_copies = {}
    scales = [1.0 / jnp.full((1, LANES), norm) for norm in norms]
    for c in chunk_order:
        rows = slice(c * chunk_rows, (c + 1) * chunk_rows)
        terms = {}
        for rank in range(CAP):
            terms[(0, 0), rank] = corrected(sources[(0, 0), rank], rows).astype(jnp.float32)
        for step in band_steps[::-1]:
            block_copies[step, c].wait_recv()
            slot = step[0] * rows_axis + step[1]
            for rank in range(CAP):
                terms[step, rank] = arrived[slot, rank, rows, :].astype(jnp.float32)

        def merged(i):
            value = corrected(under[i], rows).astype(jnp.float32)
            for key, term in terms.items():
                value = value + shares[key][i] * term
            return value * scales[i]

        for step in section_steps + [0]:
            index = lanes + offsets[step] % LANES
            turn = index & (LANES - 1)
            patch = jnp.where(
                index < LANES,
                jnp.take_along_axis(merged(2 * step), turn, axis=1),
                jnp.take_along_axis(merged(2 * step + 1), turn, axis=1),
            ).astype(jnp.bfloat16)
            if step:
                patch_out[step, rows, :] = patch
                copy = pltpu.make_async_remote_copy(
                    src_ref=patch_out.at[step, pl.ds(rows.start, chunk_rows)],
                    dst_ref=patch_in.at[step, pl.ds(rows.start, chunk_rows)],
                    send_sem=patch_send.at[step, c],
                    recv_sem=patch_recv.at[step, c],
                    device_id={"sec": slabs[step]},
                    device_id_type=MESH,
                )
                copy.start()
                patch_copies[step, c] = copy
            else:
                patch_in[0, rows, :] = patch
    jitter_out[...] = jitter_rows[...].T[0:1, :]

    table_copy.wait()
    wide = tables[0, 0:PATCH, :], tables[1, 0:PATCH, :]
    square = tables[0, PATCH : 3 * PATCH, :], tables[1, PATCH : 3 * PATCH, :]
    for step in [0] + section_steps[::-1]:
        if step:
            for c in chunk_order:
                patch_copies[step, c].wait_recv()
        source = (section - step + sections) % sections
        patch = patch_in[step]
        first = dot(patch, wide[0]) + dot(patch, wide[1])
        stacked = jnp.concatenate([first[:, :PATCH], first[:, PATCH:]], 0)
        freq[source] = dot3(square, split(stacked))

    halo.wait_send()
    for copy in list(block_copies.values()) + list(patch_copies.values()):
        copy.wait_send()


def correlate(freq, tables, jitter, jitter_out, surfaces_out):
    jitter_out[...] = jitter[...]
    wide = tables[0:PATCH, :]
    square = tables[PATCH : 3 * PATCH, :]
    for s in range(freq.shape[0] - 1):
        now_real, now_imag = freq[s, 0:PATCH], freq[s, PATCH : 2 * PATCH]
        next_real, next_imag = freq[s + 1, 0:PATCH], freq[s + 1, PATCH : 2 * PATCH]
        cross_real = now_real * next_real + now_imag * next_imag
        cross_imag = now_imag * next_real - now_real * next_imag
        magnitude = jnp.sqrt(cross_real * cross_real + cross_imag * cross_imag)
        mean = jnp.sum(jnp.sum(magnitude, axis=0, keepdims=True), axis=1, keepdims=True) * (
            1.0 / (PATCH * PATCH)
        )
        scaled = 1.0 / (magnitude + (0.5 * mean + 1e-06))
        damped = jnp.concatenate([cross_real * scaled, cross_imag * scaled], 1)
        back = dot(damped.astype(jnp.bfloat16), square)
        stacked = jnp.concatenate([back[:, :PATCH], back[:, PATCH:]], 0)
        surfaces_out[s, 0, 0] = dot(wide, stacked.astype(jnp.bfloat16)) * (1.0 / PATCH)


def per_device(section_pixels, jitter_index, drift_list, blend_weight, patch_col):
    _, row_count, row_width = section_pixels.shape
    sections = lax.axis_size("sec")
    tiles, rows_axis = lax.axis_size("tile"), lax.axis_size("row")
    owners = tiles * rows_axis
    moves = drift_list.shape[2]
    blocks = row_width // LANES
    chunks = 4
    sizes = (sections, tiles, rows_axis, row_count, row_width, moves, chunks)
    tables = dft_tables(PATCH)
    f32, bf16 = jnp.float32, jnp.bfloat16
    vmem = pl.BlockSpec(memory_space=pltpu.VMEM)
    anywhere = pl.BlockSpec(memory_space=pl.ANY)
    dma = pltpu.SemaphoreType.DMA
    jitter, freq = pl.pallas_call(
        functools.partial(kernel, sizes),
        out_shape=(
            jax.ShapeDtypeStruct((1, row_count), f32),
            jax.ShapeDtypeStruct((sections, 2 * PATCH, PATCH), f32),
        ),
        in_specs=[anywhere] * 6,
        out_specs=(vmem, vmem),
        scratch_shapes=[
            pltpu.VMEM((row_count, row_width), f32),
            pltpu.VMEM(tables.shape, bf16),
            pltpu.VMEM(jitter_index.shape, jnp.int32),
            pltpu.SMEM((1, 3, owners, moves), jnp.int32),
            pltpu.SMEM(blend_weight.shape, f32),
            pltpu.SMEM(patch_col.shape, jnp.int32),
            pltpu.VMEM((row_count, LANES), f32),
            pltpu.VMEM((blocks, row_count + 8, LANES), f32),
            pltpu.VMEM((blocks, row_count, LANES), f32),
            pltpu.VMEM((row_count, LANES), f32),
            pltpu.VMEM((row_count + 8, LANES), f32),
            pltpu.VMEM((row_count, LANES), f32),
            pltpu.VMEM((blocks, 8, LANES), f32),
            pltpu.VMEM((blocks, 1, LANES), f32),
            pltpu.VMEM((owners, CAP, BLOCK, BLOCK), bf16),
            pltpu.VMEM((owners, CAP, BLOCK, BLOCK), bf16),
            pltpu.VMEM((sections, PATCH, PATCH), bf16),
            pltpu.VMEM((sections, PATCH, PATCH), bf16),
            dma((chunks,)),
            dma,
            dma((4,)),
            dma,
            dma,
            dma((owners, chunks)),
            dma((owners, chunks)),
            dma((sections, chunks)),
            dma((sections, chunks)),
        ],
        compiler_params=pltpu.CompilerParams(collective_id=0, has_side_effects=True),
        name="section_patches",
    )(
        section_pixels,
        jitter_index,
        jnp.transpose(drift_list, (0, 3, 1, 2)),
        blend_weight,
        patch_col,
        tables,
    )
    return pl.pallas_call(
        correlate,
        out_shape=(
            jax.ShapeDtypeStruct((1, row_count), f32),
            jax.ShapeDtypeStruct((sections - 1, 1, 1, PATCH, PATCH), f32),
        ),
        in_specs=[vmem] * 3,
        out_specs=(vmem, vmem),
        name="section_correlation",
    )(freq, tables[0], jitter)


def solution(mesh):
    in_specs = (
        P(("groups", "sec"), ("tile", "row"), None),
        P(("groups", "sec"), ("tile", "row")),
        P(("groups", "sec"), None, None, None),
        P(("groups", "sec"), None, None),
        P(("tile", "row"), "groups"),
    )
    out_specs = (
        P(("groups", "sec"), ("tile", "row")),
        P("groups", ("tile", "row"), "sec", None, None),
    )
    return jax.shard_map(
        per_device, mesh=mesh, in_specs=in_specs, out_specs=out_specs, check_vma=False
    )
```

```python
import functools
import math

import jax
import jax.numpy as jnp
import numpy as np
from jax import lax
from jax.experimental import pallas as pl
from jax.experimental.pallas import tpu as pltpu
from jax.sharding import PartitionSpec as P

SEG = 512
PATCH = 128
BLOCK = 128
CAP = 2
LANES = 128
MESH = pl.DeviceIdType.MESH


def dft_tables(side):
    index = np.arange(side)
    angles = (index[:, None] * index[None, :] % side) * (2.0 * math.pi / side)
    cosine, sine = np.cos(angles), np.sin(angles)
    table = np.concatenate(
        [
            np.concatenate([cosine, sine], 1),
            np.concatenate([cosine, -sine], 1),
            np.concatenate([-sine, -cosine], 1),
        ],
        0,
    )
    high = table.astype(jnp.bfloat16)
    low = (table - high.astype(np.float64)).astype(jnp.bfloat16)
    return np.stack([high, low])


def dot(a, b):
    return jnp.dot(a, b, preferred_element_type=jnp.float32)


def split(a):
    high = a.astype(jnp.bfloat16)
    return high, (a - high.astype(jnp.float32)).astype(jnp.bfloat16)


def dot3(a, b):
    return dot(a[0], b[0]) + (dot(a[0], b[1]) + dot(a[1], b[0]))


def kernel(
    sizes,
    pixels,
    delays_hbm,
    drifts_hbm,
    weights_hbm,
    columns_hbm,
    tables_hbm,
    jitter_out,
    freq,
    tables,
    raw,
    delays,
    drifts,
    weights,
    columns,
    delay_rows,
    aligned,
    slopes,
    cross_sums,
    energies,
    jitter_rows,
    halo_out,
    halo_in,
    outbox,
    arrived,
    patch_out,
    patch_in,
    load_sem,
    table_sem,
    small_sem,
    halo_send,
    halo_recv,
    block_send,
    block_recv,
    patch_send,
    patch_recv,
):
    sections, tiles, rows_axis, row_count, row_width, moves, chunks = sizes
    owners = tiles * rows_axis
    blocks = row_width // LANES
    groups = row_count // 8
    chunk_rows = row_count // chunks
    per_seg = SEG // LANES
    tile, row_at = lax.axis_index("tile"), lax.axis_index("row")
    me = tile * rows_axis + row_at
    section = lax.axis_index("sec")

    def band_device(band):
        return {"tile": band // rows_axis, "row": band % rows_axis}

    band_steps = [(t, r) for t in range(tiles) for r in range(rows_axis)][1:]
    band_steps.sort(key=lambda step: -min(step[0], tiles - step[0]))

    def band_at(step):
        return (tile + step[0]) % tiles * rows_axis + (row_at + step[1]) % rows_axis

    def band_from(step):
        return (tile - step[0] + tiles) % tiles * rows_axis + (
            row_at - step[1] + rows_axis
        ) % rows_axis

    section_steps = sorted(range(1, sections), key=lambda step: -min(step, sections - step))

    table_copy = pltpu.make_async_copy(tables_hbm, tables, table_sem)
    loads = [
        pltpu.make_async_copy(
            pixels.at[0, pl.ds(c * chunk_rows, chunk_rows)],
            raw.at[pl.ds(c * chunk_rows, chunk_rows)],
            load_sem.at[c],
        )
        for c in range(chunks)
    ]
    small_copies = [
        pltpu.make_async_copy(source, target, small_sem.at[i])
        for i, (source, target) in enumerate(
            (
                (delays_hbm, delays),
                (drifts_hbm, drifts),
                (weights_hbm, weights),
                (columns_hbm, columns),
            )
        )
    ]
    small_copies[0].start()
    loads[chunks - 1].start()
    for c in range(chunks - 1):
        loads[c].start()
    for copy in small_copies[1:]:
        copy.start()
    table_copy.start()

    barrier = pltpu.get_barrier_semaphore()
    for step in range(1, owners):
        pl.semaphore_signal(
            barrier, inc=1, device_id=band_device((me + step) % owners), device_id_type=MESH
        )
    for step in range(1, sections):
        pl.semaphore_signal(
            barrier, inc=1, device_id={"sec": (section + step) % sections}, device_id_type=MESH
        )

    lane = lax.broadcasted_iota(jnp.int32, (8, LANES), 1)
    first_lane, last_lane = lane == 0, lane == LANES - 1
    small_copies[0].wait()
    delay_rows[...] = jnp.broadcast_to(
        delays[...].astype(jnp.float32), (LANES, row_count)
    ).T
    zero = jnp.zeros((8, LANES), jnp.float32)
    for block in range(blocks):
        aligned[block, 0:8, :] = zero

    def align(start):
        delay = delay_rows[pl.ds(start, 8), :].astype(jnp.int32)
        values = [raw[pl.ds(start, 8), v * LANES : (v + 1) * LANES] for v in range(blocks)]
        index = lane + delay
        kept = index < LANES
        index = index & (LANES - 1)
        turned = [jnp.take_along_axis(x, index, axis=1) for x in values] + [zero]
        values = [jnp.where(kept, turned[v], turned[v + 1]) for v in range(blocks)]
        return values

    def differences(values):
        before = [pltpu.roll(x, 1, 1) for x in values]
        after = [pltpu.roll(x, LANES - 1, 1) for x in values]
        line, ring = [], []
        for v in range(blocks):
            left = jnp.where(first_lane, before[v - 1] if v else zero, before[v])
            right = jnp.where(last_lane, after[v + 1] if v < blocks - 1 else zero, after[v])
            line.append(right - left)
            if v % per_seg == 0:
                left = jnp.where(first_lane, before[v + per_seg - 1], before[v])
            if v % per_seg == per_seg - 1:
                right = jnp.where(last_lane, after[v - per_seg + 1], after[v])
            ring.append(right - left)
        return line, ring

    def total(terms):
        terms = list(terms)
        while len(terms) > 1:
            terms = [
                terms[i] + terms[i + 1] if i + 1 < len(terms) else terms[i]
                for i in range(0, len(terms), 2)
            ]
        return terms[0]

    loads[chunks - 1].wait()
    last = align(row_count - 8)
    for v in range(blocks):
        halo_out[v, :, :] = last[v]
    pl.semaphore_wait(barrier, owners + sections - 2)
    halo = pltpu.make_async_remote_copy(
        src_ref=halo_out.at[:, pl.ds(7, 1)],
        dst_ref=halo_in,
        send_sem=halo_send,
        recv_sem=halo_recv,
        device_id=band_device((me + 1) % owners),
        device_id_type=MESH,
    )
    halo.start()

    def group_step(g, carry):
        start = pl.multiple_of(g * 8, 8)
        values = align(start)
        for v in range(blocks):
            aligned[v, pl.ds(start + 8, 8), :] = values[v]
        line, ring = differences(values)
        for v in range(blocks):
            slopes[v, pl.ds(start, 8), :] = 0.5 * line[v]
        energies[pl.ds(start + 8, 8), :] = total(x * x for x in values)
        cross_sums[pl.ds(start, 8), :] = total(
            aligned[v, pl.ds(start + 7, 8), :] * ring[v] for v in range(blocks)
        )
        return carry

    def find(band, owner, rank):
        source, target, weight = jnp.int32(0), jnp.int32(-1), jnp.float32(0.0)
        seen = jnp.int32(0)
        for k in range(moves):
            hit = drifts[0, 1, band, k] == owner
            here = hit & (seen == rank)
            source = jnp.where(here, drifts[0, 0, band, k], source)
            target = jnp.where(here, drifts[0, 2, band, k], target)
            weight = jnp.where(here, weights[0, band, k], weight)
            seen = seen + hit.astype(jnp.int32)
        return source, target, weight

    for copy in small_copies[1:]:
        copy.wait()
    sources = {}
    for step in band_steps + [(0, 0)]:
        for rank in range(CAP):
            sources[step, rank] = find(me, band_at(step), rank)[0]

    segs = row_width // SEG

    def corrected(block, rows):
        shifted = slice(rows.start + 8, rows.stop + 8)
        return (
            aligned[block, shifted, :] - jitter_rows[rows, :] * slopes[block, rows, :]
        ).astype(jnp.bfloat16)

    block_copies = {}

    def finish_chunk(c):
        rows = slice(c * chunk_rows, (c + 1) * chunk_rows)
        numerator = jnp.sum(cross_sums[rows, :], axis=1, keepdims=True) * (-0.5 / segs)
        power = energies[rows.start + 8 : rows.stop + 8, :]
        power = power + energies[rows.start + 7 : rows.stop + 7, :]
        power = jnp.sum(power, axis=1, keepdims=True) * (0.5 / segs)
        jitter_rows[rows, :] = jnp.broadcast_to(numerator / (power + 1e-05), (chunk_rows, LANES))
        for step in band_steps:
            slot = step[0] * rows_axis + step[1]
            for rank in range(CAP):
                outbox[slot, rank, rows, :] = corrected(sources[step, rank], rows)
            copy = pltpu.make_async_remote_copy(
                src_ref=outbox.at[slot, :, pl.ds(rows.start, chunk_rows)],
                dst_ref=arrived.at[slot, :, pl.ds(rows.start, chunk_rows)],
                send_sem=block_send.at[slot, c],
                recv_sem=block_recv.at[slot, c],
                device_id=band_device(band_at(step)),
                device_id_type=MESH,
            )
            copy.start()
            block_copies[step, c] = copy

    def finish_first():
        _, ring0 = differences([aligned[v, 8:16, :] for v in range(blocks)])
        halo.wait_recv()
        is_first = me == 0
        above = [
            jnp.where(is_first, 0.0, jnp.broadcast_to(halo_in[v], (8, LANES))) for v in range(blocks)
        ]
        row = lax.broadcasted_iota(jnp.int32, (8, LANES), 0)
        cross_sums[0:8, :] = jnp.where(
            row == 0, total(above[v] * ring0[v] for v in range(blocks)), cross_sums[0:8, :]
        )
        energies[0:8, :] = total(a * a for a in above)
        finish_chunk(0)
    per_chunk = groups // chunks
    for c in range(chunks):
        if c < chunks - 1:
            loads[c].wait()
        lax.fori_loop(c * per_chunk, (c + 1) * per_chunk, group_step, 0)
        if c:
            finish_chunk(c)
        if c == chunks - 2:
            finish_first()

    chunk_order = list(range(1, chunks - 1)) + [0, chunks - 1]

    slab_blocks = blocks // sections
    slabs = [(section + step) % sections for step in range(sections)]
    offsets = [columns[0, slab] for slab in slabs]
    under = []
    for step in range(sections):
        block = slabs[step] * slab_blocks + offsets[step] // LANES
        under += [block, jnp.minimum(block + 1, blocks - 1)]
    norms = [jnp.float32(1.0)] * len(under)
    shares = {}
    for step in [(0, 0)] + band_steps:
        for rank in range(CAP):
            _, target, weight = find(band_from(step), me, rank)
            shares[step, rank] = [jnp.where(target == block, weight, 0.0) for block in under]
            norms = [norm + share for norm, share in zip(norms, shares[step, rank])]
    lanes = lax.broadcasted_iota(jnp.int32, (chunk_rows, LANES), 1)
    patch_copies = {}
    scales = [1.0 / jnp.full((1, LANES), norm) for norm in norms]
    for c in chunk_order:
        rows = slice(c * chunk_rows, (c + 1) * chunk_rows)
        terms = {}
        for rank in range(CAP):
            terms[(0, 0), rank] = corrected(sources[(0, 0), rank], rows).astype(jnp.float32)
        for step in band_steps[::-1]:
            block_copies[step, c].wait_recv()
            slot = step[0] * rows_axis + step[1]
            for rank in range(CAP):
                terms[step, rank] = arrived[slot, rank, rows, :].astype(jnp.float32)

        def merged(i):
            value = corrected(under[i], rows).astype(jnp.float32)
            for key, term in terms.items():
                value = value + shares[key][i] * term
            return value * scales[i]

        for step in section_steps + [0]:
            index = lanes + offsets[step] % LANES
            turn = index & (LANES - 1)
            patch = jnp.where(
                index < LANES,
                jnp.take_along_axis(merged(2 * step), turn, axis=1),
                jnp.take_along_axis(merged(2 * step + 1), turn, axis=1),
            ).astype(jnp.bfloat16)
            if step:
                patch_out[step, rows, :] = patch
                copy = pltpu.make_async_remote_copy(
                    src_ref=patch_out.at[step, pl.ds(rows.start, chunk_rows)],
                    dst_ref=patch_in.at[step, pl.ds(rows.start, chunk_rows)],
                    send_sem=patch_send.at[step, c],
                    recv_sem=patch_recv.at[step, c],
                    device_id={"sec": slabs[step]},
                    device_id_type=MESH,
                )
                copy.start()
                patch_copies[step, c] = copy
            else:
                patch_in[0, rows, :] = patch
    jitter_out[...] = jitter_rows[...].T[0:1, :]

    table_copy.wait()
    wide = tables[0, 0:PATCH, :], tables[1, 0:PATCH, :]
    square = tables[0, PATCH : 3 * PATCH, :], tables[1, PATCH : 3 * PATCH, :]
    def transform(step):
        patch = patch_in[step]
        first = dot(patch, wide[0]) + dot(patch, wide[1])
        stacked = jnp.concatenate([first[:, :PATCH], first[:, PATCH:]], 0)
        freq[(section - step + sections) % sections] = dot3(square, split(stacked))

    transform(0)
    for step in section_steps[::-1]:
        for c in chunk_order:
            patch_copies[step, c].wait_recv()
    for step in section_steps[::-1]:
        transform(step)

    halo.wait_send()
    for copy in list(block_copies.values()) + list(patch_copies.values()):
        copy.wait_send()


def correlate(freq, tables, jitter, jitter_out, surfaces_out):
    jitter_out[...] = jitter[...]
    wide = tables[0, 0:PATCH, :]
    square = tables[0, PATCH : 3 * PATCH, :]
    for s in range(freq.shape[0] - 1):
        now_real, now_imag = freq[s, 0:PATCH], freq[s, PATCH : 2 * PATCH]
        next_real, next_imag = freq[s + 1, 0:PATCH], freq[s + 1, PATCH : 2 * PATCH]
        cross_real = now_real * next_real + now_imag * next_imag
        cross_imag = now_imag * next_real - now_real * next_imag
        magnitude = jnp.sqrt(cross_real * cross_real + cross_imag * cross_imag)
        mean = jnp.sum(jnp.sum(magnitude, axis=0, keepdims=True), axis=1, keepdims=True) * (
            1.0 / (PATCH * PATCH)
        )
        scaled = 1.0 / (magnitude + (0.5 * mean + 1e-06))
        damped = jnp.concatenate([cross_real * scaled, cross_imag * scaled], 1)
        back = dot(damped.astype(jnp.bfloat16), square)
        stacked = jnp.concatenate([back[:, :PATCH], back[:, PATCH:]], 0)
        surfaces_out[s, 0, 0] = dot(wide, stacked.astype(jnp.bfloat16)) * (1.0 / PATCH)


def per_device(section_pixels, jitter_index, drift_list, blend_weight, patch_col):
    _, row_count, row_width = section_pixels.shape
    sections = lax.axis_size("sec")
    tiles, rows_axis = lax.axis_size("tile"), lax.axis_size("row")
    owners = tiles * rows_axis
    moves = drift_list.shape[2]
    blocks = row_width // LANES
    chunks = 4
    sizes = (sections, tiles, rows_axis, row_count, row_width, moves, chunks)
    tables = dft_tables(PATCH)
    f32, bf16 = jnp.float32, jnp.bfloat16
    vmem = pl.BlockSpec(memory_space=pltpu.VMEM)
    anywhere = pl.BlockSpec(memory_space=pl.ANY)
    dma = pltpu.SemaphoreType.DMA
    between = pl.pallas_call(
        functools.partial(kernel, sizes),
        out_shape=(
            pltpu.VMEM((1, row_count), f32),
            pltpu.VMEM((sections, 2 * PATCH, PATCH), f32),
            pltpu.VMEM(tables.shape, bf16),
        ),
        in_specs=[anywhere] * 6,
        out_specs=(vmem, vmem, vmem),
        scratch_shapes=[
            pltpu.VMEM((row_count, row_width), f32),
            pltpu.VMEM(jitter_index.shape, jnp.int32),
            pltpu.SMEM((1, 3, owners, moves), jnp.int32),
            pltpu.SMEM(blend_weight.shape, f32),
            pltpu.SMEM(patch_col.shape, jnp.int32),
            pltpu.VMEM((row_count, LANES), f32),
            pltpu.VMEM((blocks, row_count + 8, LANES), f32),
            pltpu.VMEM((blocks, row_count, LANES), f32),
            pltpu.VMEM((row_count, LANES), f32),
            pltpu.VMEM((row_count + 8, LANES), f32),
            pltpu.VMEM((row_count, LANES), f32),
            pltpu.VMEM((blocks, 8, LANES), f32),
            pltpu.VMEM((blocks, 1, LANES), f32),
            pltpu.VMEM((owners, CAP, BLOCK, BLOCK), bf16),
            pltpu.VMEM((owners, CAP, BLOCK, BLOCK), bf16),
            pltpu.VMEM((sections, PATCH, PATCH), bf16),
            pltpu.VMEM((sections, PATCH, PATCH), bf16),
            dma((chunks,)),
            dma,
            dma((4,)),
            dma,
            dma,
            dma((owners, chunks)),
            dma((owners, chunks)),
            dma((sections, chunks)),
            dma((sections, chunks)),
        ],
        compiler_params=pltpu.CompilerParams(collective_id=0, has_side_effects=True),
        name="section_patches",
    )(
        section_pixels,
        jitter_index,
        jnp.transpose(drift_list, (0, 3, 1, 2)),
        blend_weight,
        patch_col,
        tables,
    )
    jitter, freq, tables = [pltpu.with_memory_space_constraint(x, pltpu.VMEM) for x in between]
    return pl.pallas_call(
        correlate,
        out_shape=(
            jax.ShapeDtypeStruct((1, row_count), f32),
            jax.ShapeDtypeStruct((sections - 1, 1, 1, PATCH, PATCH), f32),
        ),
        in_specs=[vmem] * 3,
        out_specs=(vmem, vmem),
        name="section_correlation",
    )(freq, tables, jitter)


def solution(mesh):
    in_specs = (
        P(("groups", "sec"), ("tile", "row"), None),
        P(("groups", "sec"), ("tile", "row")),
        P(("groups", "sec"), None, None, None),
        P(("groups", "sec"), None, None),
        P(("tile", "row"), "groups"),
    )
    out_specs = (
        P(("groups", "sec"), ("tile", "row")),
        P("groups", ("tile", "row"), "sec", None, None),
    )
    return jax.shard_map(
        per_device, mesh=mesh, in_specs=in_specs, out_specs=out_specs, check_vma=False
    )
```

```python
import functools
import math

import jax
import jax.numpy as jnp
import numpy as np
from jax import lax
from jax.experimental import pallas as pl
from jax.experimental.pallas import tpu as pltpu
from jax.sharding import PartitionSpec as P

SEG = 512
PATCH = 128
BLOCK = 128
CAP = 2
LANES = 128
MESH = pl.DeviceIdType.MESH


def dft_tables(side):
    index = np.arange(side)
    angles = (index[:, None] * index[None, :] % side) * (2.0 * math.pi / side)
    cosine, sine = np.cos(angles), np.sin(angles)
    table = np.concatenate(
        [
            np.concatenate([cosine, sine], 1),
            np.concatenate([cosine, -sine], 1),
            np.concatenate([-sine, -cosine], 1),
        ],
        0,
    )
    high = table.astype(jnp.bfloat16)
    low = (table - high.astype(np.float64)).astype(jnp.bfloat16)
    return np.stack([high, low])


def dot(a, b):
    return jnp.dot(a, b, preferred_element_type=jnp.float32)


def split(a):
    high = a.astype(jnp.bfloat16)
    return high, (a - high.astype(jnp.float32)).astype(jnp.bfloat16)


def dot3(a, b):
    return dot(a[0], b[0]) + (dot(a[0], b[1]) + dot(a[1], b[0]))


def kernel(
    sizes,
    pixels,
    delays_hbm,
    drifts_hbm,
    weights_hbm,
    columns_hbm,
    tables_hbm,
    jitter_out,
    freq,
    tables,
    raw,
    delays,
    drifts,
    weights,
    columns,
    delay_rows,
    aligned,
    slopes,
    cross_sums,
    energies,
    jitter_rows,
    halo_out,
    halo_in,
    outbox,
    arrived,
    patch_out,
    patch_in,
    load_sem,
    table_sem,
    small_sem,
    halo_send,
    halo_recv,
    block_send,
    block_recv,
    patch_send,
    patch_recv,
):
    sections, tiles, rows_axis, row_count, row_width, moves, chunks = sizes
    owners = tiles * rows_axis
    blocks = row_width // LANES
    groups = row_count // 8
    chunk_rows = row_count // chunks
    per_seg = SEG // LANES
    tile, row_at = lax.axis_index("tile"), lax.axis_index("row")
    me = tile * rows_axis + row_at
    section = lax.axis_index("sec")

    def band_device(band):
        return {"tile": band // rows_axis, "row": band % rows_axis}

    band_steps = [(t, r) for t in range(tiles) for r in range(rows_axis)][1:]
    band_steps.sort(key=lambda step: -min(step[0], tiles - step[0]))

    def band_at(step):
        return (tile + step[0]) % tiles * rows_axis + (row_at + step[1]) % rows_axis

    def band_from(step):
        return (tile - step[0] + tiles) % tiles * rows_axis + (
            row_at - step[1] + rows_axis
        ) % rows_axis

    section_steps = sorted(range(1, sections), key=lambda step: -min(step, sections - step))

    table_copy = pltpu.make_async_copy(tables_hbm, tables, table_sem)
    loads = [
        pltpu.make_async_copy(
            pixels.at[0, pl.ds(c * chunk_rows, chunk_rows)],
            raw.at[pl.ds(c * chunk_rows, chunk_rows)],
            load_sem.at[c],
        )
        for c in range(chunks)
    ]
    small_copies = [
        pltpu.make_async_copy(source, target, small_sem.at[i])
        for i, (source, target) in enumerate(
            (
                (delays_hbm, delays),
                (drifts_hbm, drifts),
                (weights_hbm, weights),
                (columns_hbm, columns),
            )
        )
    ]
    small_copies[0].start()
    loads[chunks - 1].start()
    for c in range(chunks - 1):
        loads[c].start()
    for copy in small_copies[1:]:
        copy.start()
    table_copy.start()

    barrier = pltpu.get_barrier_semaphore()
    for step in range(1, owners):
        pl.semaphore_signal(
            barrier, inc=1, device_id=band_device((me + step) % owners), device_id_type=MESH
        )
    for step in range(1, sections):
        pl.semaphore_signal(
            barrier, inc=1, device_id={"sec": (section + step) % sections}, device_id_type=MESH
        )

    lane = lax.broadcasted_iota(jnp.int32, (8, LANES), 1)
    first_lane, last_lane = lane == 0, lane == LANES - 1
    small_copies[0].wait()
    delay_rows[...] = jnp.broadcast_to(
        delays[...].astype(jnp.float32), (LANES, row_count)
    ).T
    zero = jnp.zeros((8, LANES), jnp.float32)
    for block in range(blocks):
        aligned[block, 0:8, :] = zero

    def align(start):
        delay = delay_rows[pl.ds(start, 8), :].astype(jnp.int32)
        values = [raw[pl.ds(start, 8), v * LANES : (v + 1) * LANES] for v in range(blocks)]
        index = lane + delay
        kept = index < LANES
        index = index & (LANES - 1)
        turned = [jnp.take_along_axis(x, index, axis=1) for x in values] + [zero]
        values = [jnp.where(kept, turned[v], turned[v + 1]) for v in range(blocks)]
        return values

    def differences(values):
        before = [pltpu.roll(x, 1, 1) for x in values]
        after = [pltpu.roll(x, LANES - 1, 1) for x in values]
        line, ring = [], []
        for v in range(blocks):
            left = jnp.where(first_lane, before[v - 1] if v else zero, before[v])
            right = jnp.where(last_lane, after[v + 1] if v < blocks - 1 else zero, after[v])
            line.append(right - left)
            if v % per_seg == 0:
                left = jnp.where(first_lane, before[v + per_seg - 1], before[v])
            if v % per_seg == per_seg - 1:
                right = jnp.where(last_lane, after[v - per_seg + 1], after[v])
            ring.append(right - left)
        return line, ring

    def total(terms):
        terms = list(terms)
        while len(terms) > 1:
            terms = [
                terms[i] + terms[i + 1] if i + 1 < len(terms) else terms[i]
                for i in range(0, len(terms), 2)
            ]
        return terms[0]

    loads[chunks - 1].wait()
    last = align(row_count - 8)
    for v in range(blocks):
        halo_out[v, :, :] = last[v]
    pl.semaphore_wait(barrier, owners + sections - 2)
    halo = pltpu.make_async_remote_copy(
        src_ref=halo_out.at[:, pl.ds(7, 1)],
        dst_ref=halo_in,
        send_sem=halo_send,
        recv_sem=halo_recv,
        device_id=band_device((me + 1) % owners),
        device_id_type=MESH,
    )
    halo.start()

    def group_step(g, carry):
        start = pl.multiple_of(g * 8, 8)
        values = align(start)
        for v in range(blocks):
            aligned[v, pl.ds(start + 8, 8), :] = values[v]
        line, ring = differences(values)
        for v in range(blocks):
            slopes[v, pl.ds(start, 8), :] = 0.5 * line[v]
        energies[pl.ds(start + 8, 8), :] = total(x * x for x in values)
        cross_sums[pl.ds(start, 8), :] = total(
            aligned[v, pl.ds(start + 7, 8), :] * ring[v] for v in range(blocks)
        )
        return carry

    def find(band, owner, rank):
        source, target, weight = jnp.int32(0), jnp.int32(-1), jnp.float32(0.0)
        seen = jnp.int32(0)
        for k in range(moves):
            hit = drifts[0, 1, band, k] == owner
            here = hit & (seen == rank)
            source = jnp.where(here, drifts[0, 0, band, k], source)
            target = jnp.where(here, drifts[0, 2, band, k], target)
            weight = jnp.where(here, weights[0, band, k], weight)
            seen = seen + hit.astype(jnp.int32)
        return source, target, weight

    for copy in small_copies[1:]:
        copy.wait()
    sources = {}
    for step in band_steps + [(0, 0)]:
        for rank in range(CAP):
            sources[step, rank] = find(me, band_at(step), rank)[0]

    segs = row_width // SEG

    def corrected(block, rows):
        shifted = slice(rows.start + 8, rows.stop + 8)
        return (
            aligned[block, shifted, :] - jitter_rows[rows, :] * slopes[block, rows, :]
        ).astype(jnp.bfloat16)

    block_copies = {}

    def finish_chunk(c):
        rows = slice(c * chunk_rows, (c + 1) * chunk_rows)
        numerator = jnp.sum(cross_sums[rows, :], axis=1, keepdims=True) * (-0.5 / segs)
        power = energies[rows.start + 8 : rows.stop + 8, :]
        power = power + energies[rows.start + 7 : rows.stop + 7, :]
        power = jnp.sum(power, axis=1, keepdims=True) * (0.5 / segs)
        jitter_rows[rows, :] = jnp.broadcast_to(numerator / (power + 1e-05), (chunk_rows, LANES))
        for step in band_steps:
            slot = step[0] * rows_axis + step[1]
            for rank in range(CAP):
                outbox[slot, rank, rows, :] = corrected(sources[step, rank], rows)
            copy = pltpu.make_async_remote_copy(
                src_ref=outbox.at[slot, :, pl.ds(rows.start, chunk_rows)],
                dst_ref=arrived.at[slot, :, pl.ds(rows.start, chunk_rows)],
                send_sem=block_send.at[slot, c],
                recv_sem=block_recv.at[slot, c],
                device_id=band_device(band_at(step)),
                device_id_type=MESH,
            )
            copy.start()
            block_copies[step, c] = copy

    def finish_first():
        _, ring0 = differences([aligned[v, 8:16, :] for v in range(blocks)])
        halo.wait_recv()
        is_first = me == 0
        above = [
            jnp.where(is_first, 0.0, jnp.broadcast_to(halo_in[v], (8, LANES))) for v in range(blocks)
        ]
        row = lax.broadcasted_iota(jnp.int32, (8, LANES), 0)
        cross_sums[0:8, :] = jnp.where(
            row == 0, total(above[v] * ring0[v] for v in range(blocks)), cross_sums[0:8, :]
        )
        energies[0:8, :] = total(a * a for a in above)
        finish_chunk(0)
    per_chunk = groups // chunks
    for c in range(chunks):
        if c < chunks - 1:
            loads[c].wait()
        lax.fori_loop(c * per_chunk, (c + 1) * per_chunk, group_step, 0)
        if c:
            finish_chunk(c)
        if c == chunks - 2:
            finish_first()

    chunk_order = list(range(1, chunks - 1)) + [0, chunks - 1]

    slab_blocks = blocks // sections
    slabs = [(section + step) % sections for step in range(sections)]
    offsets = [columns[0, slab] for slab in slabs]
    under = []
    for step in range(sections):
        block = slabs[step] * slab_blocks + offsets[step] // LANES
        under += [block, jnp.minimum(block + 1, blocks - 1)]
    norms = [jnp.float32(1.0)] * len(under)
    shares = {}
    for step in [(0, 0)] + band_steps:
        for rank in range(CAP):
            _, target, weight = find(band_from(step), me, rank)
            shares[step, rank] = [jnp.where(target == block, weight, 0.0) for block in under]
            norms = [norm + share for norm, share in zip(norms, shares[step, rank])]
    lanes = lax.broadcasted_iota(jnp.int32, (chunk_rows, LANES), 1)
    patch_copies = {}
    scales = [1.0 / jnp.full((1, LANES), norm) for norm in norms]
    for c in chunk_order:
        rows = slice(c * chunk_rows, (c + 1) * chunk_rows)
        terms = {}
        for rank in range(CAP):
            terms[(0, 0), rank] = corrected(sources[(0, 0), rank], rows).astype(jnp.float32)
        for step in band_steps[::-1]:
            block_copies[step, c].wait_recv()
            slot = step[0] * rows_axis + step[1]
            for rank in range(CAP):
                terms[step, rank] = arrived[slot, rank, rows, :].astype(jnp.float32)

        def merged(i):
            value = corrected(under[i], rows).astype(jnp.float32)
            for key, term in terms.items():
                value = value + shares[key][i] * term
            return value * scales[i]

        for step in section_steps + [0]:
            index = lanes + offsets[step] % LANES
            turn = index & (LANES - 1)
            patch = jnp.where(
                index < LANES,
                jnp.take_along_axis(merged(2 * step), turn, axis=1),
                jnp.take_along_axis(merged(2 * step + 1), turn, axis=1),
            ).astype(jnp.bfloat16)
            if step:
                patch_out[step, rows, :] = patch
                copy = pltpu.make_async_remote_copy(
                    src_ref=patch_out.at[step, pl.ds(rows.start, chunk_rows)],
                    dst_ref=patch_in.at[step, pl.ds(rows.start, chunk_rows)],
                    send_sem=patch_send.at[step, c],
                    recv_sem=patch_recv.at[step, c],
                    device_id={"sec": slabs[step]},
                    device_id_type=MESH,
                )
                copy.start()
                patch_copies[step, c] = copy
            else:
                patch_in[0, rows, :] = patch
    jitter_out[...] = jitter_rows[...].T[0:1, :]

    table_copy.wait()
    wide = tables[0, 0:PATCH, :], tables[1, 0:PATCH, :]
    square = tables[0, PATCH : 3 * PATCH, :], tables[1, PATCH : 3 * PATCH, :]
    def transform(steps):
        patches = jnp.concatenate([patch_in[step] for step in steps], 0)
        first = dot(patches, wide[0]) + dot(patches, wide[1])
        stacked = [
            jnp.concatenate([first[at : at + PATCH, :PATCH], first[at : at + PATCH, PATCH:]], 0)
            for at in range(0, len(steps) * PATCH, PATCH)
        ]
        both = dot3(square, split(jnp.concatenate(stacked, 1)))
        for i, step in enumerate(steps):
            source = (section - step + sections) % sections
            freq[source] = both[:, i * PATCH : (i + 1) * PATCH]

    transform([0])
    for step in section_steps[::-1]:
        for c in chunk_order:
            patch_copies[step, c].wait_recv()
    transform(section_steps[::-1])

    halo.wait_send()
    for copy in list(block_copies.values()) + list(patch_copies.values()):
        copy.wait_send()


def correlate(freq, tables, jitter, jitter_out, surfaces_out):
    jitter_out[...] = jitter[...]
    wide = tables[0, 0:PATCH, :]
    square = tables[0, PATCH : 3 * PATCH, :]
    for s in range(freq.shape[0] - 1):
        now_real, now_imag = freq[s, 0:PATCH], freq[s, PATCH : 2 * PATCH]
        next_real, next_imag = freq[s + 1, 0:PATCH], freq[s + 1, PATCH : 2 * PATCH]
        cross_real = now_real * next_real + now_imag * next_imag
        cross_imag = now_imag * next_real - now_real * next_imag
        magnitude = jnp.sqrt(cross_real * cross_real + cross_imag * cross_imag)
        mean = jnp.sum(jnp.sum(magnitude, axis=0, keepdims=True), axis=1, keepdims=True) * (
            1.0 / (PATCH * PATCH)
        )
        scaled = 1.0 / (magnitude + (0.5 * mean + 1e-06))
        damped = jnp.concatenate([cross_real * scaled, cross_imag * scaled], 1)
        back = dot(damped.astype(jnp.bfloat16), square)
        stacked = jnp.concatenate([back[:, :PATCH], back[:, PATCH:]], 0)
        surfaces_out[s, 0, 0] = dot(wide, stacked.astype(jnp.bfloat16)) * (1.0 / PATCH)


def per_device(section_pixels, jitter_index, drift_list, blend_weight, patch_col):
    _, row_count, row_width = section_pixels.shape
    sections = lax.axis_size("sec")
    tiles, rows_axis = lax.axis_size("tile"), lax.axis_size("row")
    owners = tiles * rows_axis
    moves = drift_list.shape[2]
    blocks = row_width // LANES
    chunks = 4
    sizes = (sections, tiles, rows_axis, row_count, row_width, moves, chunks)
    tables = dft_tables(PATCH)
    f32, bf16 = jnp.float32, jnp.bfloat16
    vmem = pl.BlockSpec(memory_space=pltpu.VMEM)
    anywhere = pl.BlockSpec(memory_space=pl.ANY)
    dma = pltpu.SemaphoreType.DMA
    between = pl.pallas_call(
        functools.partial(kernel, sizes),
        out_shape=(
            pltpu.VMEM((1, row_count), f32),
            pltpu.VMEM((sections, 2 * PATCH, PATCH), f32),
            pltpu.VMEM(tables.shape, bf16),
        ),
        in_specs=[anywhere] * 6,
        out_specs=(vmem, vmem, vmem),
        scratch_shapes=[
            pltpu.VMEM((row_count, row_width), f32),
            pltpu.VMEM(jitter_index.shape, jnp.int32),
            pltpu.SMEM((1, 3, owners, moves), jnp.int32),
            pltpu.SMEM(blend_weight.shape, f32),
            pltpu.SMEM(patch_col.shape, jnp.int32),
            pltpu.VMEM((row_count, LANES), f32),
            pltpu.VMEM((blocks, row_count + 8, LANES), f32),
            pltpu.VMEM((blocks, row_count, LANES), f32),
            pltpu.VMEM((row_count, LANES), f32),
            pltpu.VMEM((row_count + 8, LANES), f32),
            pltpu.VMEM((row_count, LANES), f32),
            pltpu.VMEM((blocks, 8, LANES), f32),
            pltpu.VMEM((blocks, 1, LANES), f32),
            pltpu.VMEM((owners, CAP, BLOCK, BLOCK), bf16),
            pltpu.VMEM((owners, CAP, BLOCK, BLOCK), bf16),
            pltpu.VMEM((sections, PATCH, PATCH), bf16),
            pltpu.VMEM((sections, PATCH, PATCH), bf16),
            dma((chunks,)),
            dma,
            dma((4,)),
            dma,
            dma,
            dma((owners, chunks)),
            dma((owners, chunks)),
            dma((sections, chunks)),
            dma((sections, chunks)),
        ],
        compiler_params=pltpu.CompilerParams(collective_id=0, has_side_effects=True),
        name="section_patches",
    )(
        section_pixels,
        jitter_index,
        jnp.transpose(drift_list, (0, 3, 1, 2)),
        blend_weight,
        patch_col,
        tables,
    )
    jitter, freq, tables = [pltpu.with_memory_space_constraint(x, pltpu.VMEM) for x in between]
    return pl.pallas_call(
        correlate,
        out_shape=(
            jax.ShapeDtypeStruct((1, row_count), f32),
            jax.ShapeDtypeStruct((sections - 1, 1, 1, PATCH, PATCH), f32),
        ),
        in_specs=[vmem] * 3,
        out_specs=(vmem, vmem),
        name="section_correlation",
    )(freq, tables, jitter)


def solution(mesh):
    in_specs = (
        P(("groups", "sec"), ("tile", "row"), None),
        P(("groups", "sec"), ("tile", "row")),
        P(("groups", "sec"), None, None, None),
        P(("groups", "sec"), None, None),
        P(("tile", "row"), "groups"),
    )
    out_specs = (
        P(("groups", "sec"), ("tile", "row")),
        P("groups", ("tile", "row"), "sec", None, None),
    )
    return jax.shard_map(
        per_device, mesh=mesh, in_specs=in_specs, out_specs=out_specs, check_vma=False
    )
```
